256 devices in a mesh: track: 16 (over x, y), lateral: 8 (over z_lo, core), depth: 2 (over z_hi).
Axes of the slice: x: 4, y: 4, z: 8 (z_hi: 2, z_lo: 4; z = z_hi * 4 + z_lo), core: 2. Of those that a mesh axis runs over, the one named last changes fastest.
Arguments:
- rhs: float32 [128, 16, 2, 64, 256], P('track', 'lateral', None, None, 'depth'), may hold values from -6 to 6
- start: float32 [128, 16, 2, 64, 256], P('track', 'lateral', None, None, 'depth'), may hold values from -6 to 6
- fine_blocks: bfloat16 [128, 16, 2, 27, 4096], P('track', 'lateral'), may hold values from -0.15625 to 0.15625
- fine_cols: int32 [128, 16, 2, 27], P('track', 'lateral'), may hold values from 0 to 26, each once within a row
- fine_mass: bfloat16 [128, 16, 2, 64], P('track', 'lateral'), may hold values from 4 to 8
- fine_smoother: bfloat16 [128, 16, 2, 4096], P('track', 'lateral'), may hold values from -0.05 to 0.25
- transfer: bfloat16 [128, 16, 2, 4096], P('track', 'lateral'), may hold values from -0.75 to 0.75
- aggregate: int32 [128, 16, 2], P('track', 'lateral'), may hold values from 0 to 127, as said below
- coarse_blocks: bfloat16 [128, 8, 2, 27, 4096], P(('track', 'lateral'), None, 'depth'), may hold values from -0.15625 to 0.15625
- coarse_cols: int32 [128, 8, 2, 27], P(('track', 'lateral'), None, 'depth'), may hold values from 0 to 26, each once within a row
- coarse_mass: bfloat16 [128, 8, 2, 64], P(('track', 'lateral'), None, 'depth'), may hold values from 1.5 to 3
- coarse_smoother: bfloat16 [128, 8, 2, 4096], P(('track', 'lateral'), None, 'depth'), may hold values from -0.2 to 1
Outputs:
- solution: float32 [128, 16, 2, 64, 256], P('track', 'lateral', None, None, 'depth')
The draws below stay inside these ranges and needn't reach their ends.
Inputs may be any that keep to these rules, and one draw needn't show every extreme that they name: `fine_cols`: each row lists every neighbour code once. `coarse_cols`: each row lists every neighbour code once. `aggregate`: for every y and z, the entries at x = 8 * q to 8 * q + 7 are a permutation of those same x.
All inputs are finite; a program needn't handle non-finite values.
Results may differ from the reference program's by a relative error of at most 0.01.
The reference program's roundings to bfloat16 on the way (of `correction`) count: a program that leaves them out, or rounds other values in their place, can miss the bound.
Values may be sent and summed in bfloat16 or wider, within the bound.
A program may use at most 128 MiB of HBM per device.

```python
import math
import jax
import jax.numpy as jnp
from jax import lax

B = 64
FX = 8
NZ = 2
SWEEPS = 2
NX = 128
NY = 16
CY = 8
LOADS = 256


def smoother_values(key, shape, width, centre_lo, centre_hi, spread):
    first_key, second_key = jax.random.split(key)
    centre = jax.random.uniform(first_key, shape, jnp.float32, centre_lo, centre_hi)
    noise = spread * jax.random.normal(second_key, shape, jnp.float32)
    noise = jnp.clip(noise, -4.0 * spread, 4.0 * spread)
    position = jnp.arange(width * width, dtype=jnp.int32)
    on_diagonal = position // width == position % width
    return jnp.where(on_diagonal, centre, noise)


def draw_fine_smoother(key, part):
    return smoother_values(key, (NX, NY, NZ, B * B), B, 0.12, 0.2, 0.005).astype(jnp.bfloat16)


def draw_coarse_smoother(key, part):
    return smoother_values(key, (NX, NY // 2, NZ, B * B), B, 0.3, 0.5, 0.015).astype(jnp.bfloat16)


def draw_aggregate(key, part):
    blocks_x = NX // FX
    scores = jax.random.randint(key, (blocks_x, FX, NY, NZ), 0, 1 << 20, dtype=jnp.int32)
    scores = scores * FX + jnp.arange(FX, dtype=jnp.int32)[None, :, None, None]
    ranking = jnp.argsort(scores, axis=1, stable=True).astype(jnp.int32)
    starts = (jnp.arange(blocks_x, dtype=jnp.int32) * FX)[:, None, None, None]
    return (ranking + starts).reshape(NX, NY, NZ).astype(jnp.int32)


def steps_of(own_key, dims, shards, least, largest):
    level, own = 1.0, jax.random.fold_in(own_key, 6)
    for dim, blocks in shards:
        steps = jnp.exp(jax.random.uniform(jax.random.fold_in(own, dim), (blocks,), jnp.float32, least / len(shards), largest / len(shards)))
        level = level * jnp.repeat(steps, dims[dim] // blocks).reshape([-1 if axis == dim else 1 for axis in range(len(dims))])
    return level


def scatter_about(stream_key, shape, deviation, most, shards=(), kind=jnp.bfloat16):
    drawn = jax.random.normal(stream_key, shape, jnp.float32) * deviation
    if len(shards) > 0:
        drawn = steps_of(stream_key, shape, shards, -0.22, 0.18) * drawn
    return jnp.clip(drawn, min=-most, max=most).astype(kind)


def setup_inputs(seed: int = 0) -> dict:
    splits = jax.random.split(jax.random.key(seed), 13)
    return {
        "rhs": scatter_about(splits[0], (NX, NY, NZ, B, LOADS), 1.0, 6.0, ((0, 16), (1, 8), (4, 2)), jnp.float32),
        "start": scatter_about(splits[1], (NX, NY, NZ, B, LOADS), 1.0, 6.0, ((0, 16), (1, 8), (4, 2)), jnp.float32),
        "fine_blocks": scatter_about(splits[2], (NX, NY, NZ, 27, B * B), (27 * B) ** -0.5, 0.15625, ((0, 16), (1, 8))),
        "fine_cols": jax.vmap(lambda own: jax.random.permutation(own, 27))(jax.random.split(splits[3], NX * NY * NZ)).reshape((NX, NY, NZ, 27)).astype(jnp.int32),
        "fine_mass": jnp.clip(jnp.exp(math.log(8.0) - 0.6931472 * jax.random.uniform(splits[4], (NX, NY, NZ, B), jnp.float32) ** steps_of(splits[4], (NX, NY, NZ, B), ((0, 16), (1, 8)), -0.2, 0.2)), 4.0, 8.0).astype(jnp.bfloat16),
        "fine_smoother": draw_fine_smoother(jax.random.fold_in(splits[12], 71), 0),
        "transfer": scatter_about(splits[6], (NX, NY, NZ, B * B), B ** -0.5, 0.75, ((0, 16), (1, 8))),
        "aggregate": draw_aggregate(jax.random.fold_in(splits[12], 71), 0),
        "coarse_blocks": scatter_about(splits[8], (NX, CY, NZ, 27, B * B), (27 * B) ** -0.5, 0.15625, ((0, 128), (2, 2))),
        "coarse_cols": jax.vmap(lambda own: jax.random.permutation(own, 27))(jax.random.split(splits[9], NX * CY * NZ)).reshape((NX, CY, NZ, 27)).astype(jnp.int32),
        "coarse_mass": jnp.clip(jnp.exp(math.log(3.0) - 0.6931472 * jax.random.uniform(splits[10], (NX, CY, NZ, B), jnp.float32) ** steps_of(splits[10], (NX, CY, NZ, B), ((0, 128), (2, 2)), -0.2, 0.2)), 1.5, 3.0).astype(jnp.bfloat16),
        "coarse_smoother": draw_coarse_smoother(jax.random.fold_in(splits[12], 71), 0),
    }


damping = 0.8


def offset_slots(lists):
    codes = jnp.arange(27, dtype=jnp.int32)
    match = lists[..., :, None] == codes
    return jnp.sum(jnp.where(match, codes[:, None], 0), axis=-2).astype(jnp.int32)


def sort_blocks(blocks, lists, width):
    slots = offset_slots(lists)
    taken = jnp.take_along_axis(blocks, slots[..., None], axis=3)
    return taken.reshape(blocks.shape[:3] + (27, width, width))


def round_keep(values):
    return lax.optimization_barrier(values.astype(jnp.bfloat16))


def apply_operator(sorted_ops, mass, rounded):
    size_x, size_y, size_z = rounded.shape[:3]
    padded = jnp.pad(rounded, ((1, 1), (1, 1), (1, 1), (0, 0), (0, 0)))
    total = mass.astype(jnp.float32)[..., None] * rounded.astype(jnp.float32)
    for offset in range(27):
        along_x = offset // 9
        along_y = (offset // 3) % 3
        along_z = offset % 3
        piece = padded[along_x:along_x + size_x, along_y:along_y + size_y, along_z:along_z + size_z]
        total = total + jnp.einsum("xyzij,xyzjk->xyzik", sorted_ops[:, :, :, offset].astype(jnp.float32),
                                   piece.astype(jnp.float32), precision=lax.Precision.HIGHEST)
    return total


def smooth_step(smoother, residual, width):
    mats = smoother.reshape(smoother.shape[:3] + (width, width)).astype(jnp.float32)
    rounded = residual.astype(jnp.bfloat16).astype(jnp.float32)
    return damping * jnp.einsum("xyzij,xyzjk->xyzik", mats, rounded, precision=lax.Precision.HIGHEST)


def reference(rhs, start, fine_blocks, fine_cols, fine_mass, fine_smoother, transfer, aggregate,
              coarse_blocks, coarse_cols, coarse_mass, coarse_smoother):
    sorted_fine = sort_blocks(fine_blocks, fine_cols, B)
    iterate = start
    for sweep in range(SWEEPS):
        rounded = round_keep(iterate)
        fine_res = rhs - apply_operator(sorted_fine, fine_mass, rounded)
        iterate = iterate + smooth_step(fine_smoother, fine_res, B)
    rounded = round_keep(iterate)
    residual = rhs - apply_operator(sorted_fine, fine_mass, rounded)
    mats = transfer.reshape(transfer.shape[:3] + (B, B)).astype(jnp.float32)
    projected = jnp.einsum("xyzji,xyzjk->xyzik", mats, residual.astype(jnp.bfloat16).astype(jnp.float32),
                           precision=lax.Precision.HIGHEST)
    blocks_x = NX // FX
    starts = (jnp.arange(blocks_x, dtype=jnp.int32) * FX)[:, None, None, None]
    local = aggregate.reshape(blocks_x, FX, NY, NZ) - starts
    local = local.reshape(blocks_x, FX, NY // 2, 2, NZ)
    targets = jnp.arange(FX, dtype=jnp.int32)[None, :, None, None, None, None]
    selector = (local[:, None] == targets).astype(jnp.float32)
    grouped = projected.reshape(blocks_x, FX, NY // 2, 2, NZ, B, LOADS)
    coarse_res = jnp.einsum("nuxyvz,nxyvzik->nuyzik", selector, grouped, precision=lax.Precision.HIGHEST)
    coarse_res = coarse_res.reshape(NX, NY // 2, NZ, B, LOADS)
    sorted_coarse = sort_blocks(coarse_blocks, coarse_cols, B)
    first = smooth_step(coarse_smoother, coarse_res, B)
    first_round = round_keep(first)
    remain = coarse_res - apply_operator(sorted_coarse, coarse_mass, first_round)
    correction = (first + smooth_step(coarse_smoother, remain, B)).astype(jnp.bfloat16)
    spread = jnp.einsum("nuxyvz,nuyzik->nxyvzik", selector,
                        correction.astype(jnp.float32).reshape(blocks_x, FX, NY // 2, NZ, B, LOADS),
                        precision=lax.Precision.HIGHEST)
    spread = spread.reshape(NX, NY, NZ, B, LOADS)
    added = jnp.einsum("xyzij,xyzjk->xyzik", mats, spread, precision=lax.Precision.HIGHEST)
    return iterate + added
```

```python
import functools

import jax
import jax.numpy as jnp
from jax import lax
from jax.experimental import pallas as pl
from jax.experimental.pallas import tpu as pltpu
from jax.sharding import PartitionSpec as P

SWEEPS = 2
DAMPING = 0.8
B = 64
H = B // 2
COLS = B * B
TILES = COLS // 128
CODES = 27
LD = 128
WIDE = 10 * 128
F32 = jnp.float32
BF16 = jnp.bfloat16
MESH = pl.DeviceIdType.MESH
STEPS = [(0, -1), (0, 1), (-1, 0), (1, 0), (-1, -1), (-1, 1), (1, -1), (1, 1)]


def lanes_low(rows):
    return lax.broadcasted_iota(jnp.int32, (rows, 128), 1) < B


def even_odd(low, first, second):
    even = jnp.where(low, first, pltpu.roll(second, B, 1))
    odd = jnp.where(low, pltpu.roll(first, B, 1), second)
    return even, odd


def spread_slots(blocks, spread):
    for group in range(0, CODES, 8):
        rows = min(8, CODES - group)
        for tile in range(TILES):
            at = group * TILES + tile * 8
            piece = blocks[pl.ds(group, rows), pl.ds(tile * 128, 128)]
            spread[pl.ds(at, rows), :] = piece.astype(F32)


def slot_start(slot):
    return (slot // 8) * (8 * TILES) + slot % 8


def mass_rows(mass, parity, layer):
    row = lax.broadcasted_iota(jnp.int32, (H, B), 0) * 2 + parity
    col = lax.broadcasted_iota(jnp.int32, (H, B), 1)
    diag = jnp.where(row == col, jnp.broadcast_to(mass, (H, B)), 0.0)
    zero = jnp.zeros((H, B), F32)
    return jnp.concatenate([diag, zero] if layer == 0 else [zero, diag], axis=1)


def prep_kernel(
    fcols, ccols, agg, fblk, fmass, fsm, tran, cblk, cmass, csm,
    fine, smooth, transfer, coarse, csmooth, inverse,
    spread, few, slots,
):
    step = pl.program_id(0)
    x = step // 2
    y = step % 2
    size_x = agg.shape[0]
    low = lanes_low(H)

    for layer in range(2):
        for k in range(CODES):
            slots[layer * CODES + fcols[x, y, layer, k]] = k
        spread_slots(fblk.at[0, 0, layer], spread.at[layer])
    for layer in range(2):
        for near in range(9):
            code = near * 3 + 1 - layer
            parts = []
            for z in range(2):
                start = slot_start(slots[layer * CODES + code + z])
                parts.append(spread[layer, pl.ds(start, TILES, stride=8), :])
            even, odd = even_odd(low, *parts)
            at = pl.ds(near * 128, 128)
            fine[0, pl.ds(layer * B, H), at] = even.astype(BF16)
            fine[0, pl.ds(layer * B + H, H), at] = odd.astype(BF16)
        for parity in range(2):
            rows = mass_rows(fmass[0, 0, pl.ds(layer, 1), :].astype(F32), parity, layer)
            fine[0, pl.ds(layer * B + parity * H, H), pl.ds(9 * 128, 128)] = rows.astype(BF16)

    for source, target in ((fsm, smooth), (tran, transfer)):
        for tile in range(TILES):
            piece = source[0, 0, :, pl.ds(tile * 128, 128)]
            few[pl.ds(tile * 8, 2), :] = piece.astype(F32)
        for layer in range(2):
            block = few[pl.ds(layer, TILES, stride=8), :]
            zero = jnp.zeros_like(block)
            pair = (block, zero) if layer == 0 else (zero, block)
            even, odd = even_odd(low, *pair)
            target[0, pl.ds(layer * B, H), :] = even.astype(BF16)
            target[0, pl.ds(layer * B + H, H), :] = odd.astype(BF16)

    @pl.when(y == 0)
    def _():
        depth = lax.axis_index("depth")
        for k in range(CODES):
            slots[ccols[0, x, 0, k]] = k
        spread_slots(cblk.at[0, 0, 0], spread.at[0])
        for near in range(9):
            parts = []
            for z in range(2):
                start = slot_start(slots[near * 3 + 1 + z - depth])
                parts.append(spread[0, pl.ds(start, TILES, stride=8), :])
            even, odd = even_odd(low, *parts)
            at = pl.ds(near * 128, 128)
            coarse[0, pl.ds(0, H), at] = even.astype(BF16)
            coarse[0, pl.ds(H, H), at] = odd.astype(BF16)
        mine = lax.broadcasted_iota(jnp.int32, (H, 128), 1) // B == depth
        for parity in range(2):
            mass = cmass[0, 0, pl.ds(0, 1), :].astype(F32)
            rows = mass_rows(mass, parity, 0)
            rows = jnp.where(mine, rows + pltpu.roll(rows, B, 1), 0.0)
            coarse[0, pl.ds(parity * H, H), pl.ds(9 * 128, 128)] = rows.astype(BF16)

    @pl.when(step == 0)
    def _():
        count = csm.shape[1]
        for row in range(count):
            for tile in range(TILES):
                piece = csm[0, row, pl.ds(0, 1), pl.ds(tile * 128, 128)]
                few[pl.ds(tile * 8 + row, 1), :] = piece.astype(F32)
        for pair in range(count // 2):
            parts = [few[pl.ds(2 * pair + k, TILES, stride=8), :] for k in range(2)]
            even, odd = even_odd(low, *parts)
            csmooth[pair, pl.ds(0, H), :] = even.astype(BF16)
            csmooth[pair, pl.ds(H, H), :] = odd.astype(BF16)
        for side in range(2):
            for layer in range(2):
                for place in range(size_x):
                    at = (side * 2 + layer) * size_x + lax.rem(agg[place, side, layer], size_x)
                    inverse[at] = place


def prepare(fine_blocks, fine_cols, fine_mass, fine_smoother, transfer, aggregate,
            coarse_blocks, coarse_cols, coarse_mass, coarse_smoother):
    size_x = fine_blocks.shape[0]
    count = 2 * size_x
    whole = pl.BlockSpec(memory_space=pltpu.SMEM)

    def per_xy(*rest):
        zeros = (0,) * len(rest)
        return pl.BlockSpec((1, 1) + rest, lambda i: (i // 2, i % 2) + zeros)

    def per_y(*rest):
        zeros = (0,) * len(rest)
        return pl.BlockSpec((1, 1) + rest, lambda i: (0, i // 2) + zeros)

    return pl.pallas_call(
        prep_kernel,
        grid=(count,),
        in_specs=[
            whole, whole, whole,
            per_xy(2, CODES, COLS), per_xy(2, B), per_xy(2, COLS), per_xy(2, COLS),
            per_y(1, CODES, COLS), per_y(1, B),
            pl.BlockSpec(coarse_smoother.shape, lambda i: (0, 0, 0, 0)),
        ],
        out_specs=[
            pl.BlockSpec((1, 128, WIDE), lambda i: (i, 0, 0)),
            pl.BlockSpec((1, 128, 128), lambda i: (i, 0, 0)),
            pl.BlockSpec((1, 128, 128), lambda i: (i, 0, 0)),
            pl.BlockSpec((1, B, WIDE), lambda i: (i // 2, 0, 0)),
            pl.BlockSpec((size_x // 2, B, 128), lambda i: (0, 0, 0)),
            whole,
        ],
        out_shape=[
            jax.ShapeDtypeStruct((count, 128, WIDE), BF16),
            jax.ShapeDtypeStruct((count, 128, 128), BF16),
            jax.ShapeDtypeStruct((count, 128, 128), BF16),
            jax.ShapeDtypeStruct((size_x, B, WIDE), BF16),
            jax.ShapeDtypeStruct((size_x // 2, B, 128), BF16),
            jax.ShapeDtypeStruct((4 * size_x,), jnp.int32),
        ],
        scratch_shapes=[
            pltpu.VMEM((2, 32 * TILES, 128), F32),
            pltpu.VMEM((8 * TILES, 128), F32),
            pltpu.SMEM((2 * CODES,), jnp.int32),
        ],
        compiler_params=pltpu.CompilerParams(vmem_limit_bytes=32 << 20),
        name="prepare",
    )(fine_cols, coarse_cols, aggregate, fine_blocks, fine_mass, fine_smoother, transfer,
      coarse_blocks, coarse_mass, coarse_smoother)


def dot(left, right):
    return jnp.dot(left, right, preferred_element_type=F32)


def every_second(parity):
    return pl.ds(parity, H, stride=2)


def cycle_kernel(
    tracks, agg, inverse, rhs, start, fine, smooth, transfer, coarse, csmooth,
    out,
    padded, iterate, natural, projected, csend, cres, cpad, call, first, csend_back, corr,
    cnatural,
    halo_send, halo_recv, to_send, to_recv, back_send, back_recv, side_send, side_recv,
    ss_send, ss_recv,
):
    size_x = rhs.shape[0]
    size_l = size_x
    track = lax.axis_index("track")
    lateral = lax.axis_index("lateral")
    depth = lax.axis_index("depth")
    group = 2 * size_l
    me = lateral * 2 + depth

    def exists(dt, dl):
        ok = None
        for step, at, count in ((dt, track, tracks), (dl, lateral, size_l)):
            if step:
                here = (at > 0) if step < 0 else (at < count - 1)
                ok = here if ok is None else jnp.logical_and(ok, here)
        return ok

    def ring(r):
        other = lax.rem(me + r, group)
        return other // 2, lax.rem(other, 2)

    last = size_l - 1
    before = (track - (lateral == 0).astype(jnp.int32), lax.rem(lateral + last, size_l), depth)
    after = (track + (lateral == last).astype(jnp.int32), lax.rem(lateral + 1, size_l), depth)
    sides = (
        (before, jnp.logical_or(track > 0, lateral > 0)),
        (after, jnp.logical_or(track < tracks - 1, lateral < last)),
    )

    for sweep in range(SWEEPS + 1):
        for place in (0, size_x + 1):
            padded[sweep, place] = jnp.zeros_like(padded[sweep, place])
        for place in (0, 3):
            padded[sweep, :, place] = jnp.zeros_like(padded[sweep, :, place])
    for place in (0, 2):
        cpad[place] = jnp.zeros_like(cpad[place])
    for place in (0, size_l + 1):
        cpad[1, :, place] = jnp.zeros_like(cpad[1, :, place])

    barrier = pltpu.get_barrier_semaphore()
    for r in range(1, group):
        other_l, other_d = ring(r)
        pl.semaphore_signal(barrier, inc=1, device_id=(track, other_l, other_d), device_id_type=MESH)
    expected = group - 1
    for dt, dl in STEPS:
        if dt:
            ok = exists(dt, dl)

            @pl.when(ok)
            def _(dt=dt, dl=dl):
                pl.semaphore_signal(
                    barrier, inc=1, device_id=(track + dt, lateral + dl, depth), device_id_type=MESH
                )

            expected = expected + ok.astype(jnp.int32)
    for (device, ok), at_end in zip(sides, (lateral == 0, lateral == last)):
        crossing = jnp.logical_and(ok, at_end)

        @pl.when(crossing)
        def _(device=device):
            pl.semaphore_signal(barrier, inc=1, device_id=device, device_id_type=MESH)

        expected = expected + crossing.astype(jnp.int32)

    def round_start(x, carry):
        for y in range(2):
            for z in range(2):
                padded[0, x + 1, y + 1, pl.ds(z * B, B), :] = start[x, y, z].astype(BF16)
        return carry

    lax.fori_loop(0, size_x, round_start, 0)
    pl.semaphore_wait(barrier, expected)

    def halo_copy(sweep, index):
        dt, dl = STEPS[index]
        src_x, dst_x = {0: (pl.ds(1, size_x),) * 2, -1: (1, size_x + 1), 1: (size_x, 0)}[dt]
        src_y, dst_y = {0: (pl.ds(1, 2),) * 2, -1: (1, 3), 1: (2, 0)}[dl]
        return pltpu.make_async_remote_copy(
            src_ref=padded.at[sweep, src_x, src_y],
            dst_ref=padded.at[sweep, dst_x, dst_y],
            send_sem=halo_send.at[sweep, index],
            recv_sem=halo_recv.at[sweep, index],
            device_id=(track + dt, lateral + dl, depth),
            device_id_type=MESH,
        )

    def halo_start(sweep):
        for index, (dt, dl) in enumerate(STEPS):
            @pl.when(exists(dt, dl))
            def _(index=index):
                halo_copy(sweep, index).start()

    def halo_wait(sweep):
        for index, (dt, dl) in enumerate(STEPS):
            @pl.when(exists(-dt, -dl))
            def _(index=index):
                halo_copy(sweep, index).wait_recv()

            @pl.when(exists(dt, dl))
            def _(index=index):
                halo_copy(sweep, index).wait_send()

    halo_start(0)
    call[depth] = csmooth[...]
    partner = pltpu.make_async_remote_copy(
        src_ref=call.at[depth],
        dst_ref=call.at[depth],
        send_sem=ss_send,
        recv_sem=ss_recv,
        device_id=(track, lateral, 1 - depth),
        device_id_type=MESH,
    )
    partner.start()

    def apply_fine(sweep, x, y):
        pieces = [
            padded[sweep, x + dx, pl.ds(y, 3)].reshape(3 * 128, LD) for dx in range(3)
        ]
        pieces.append(padded[sweep, x + 1, y + 1])
        return dot(fine[2 * x + y], jnp.concatenate(pieces, axis=0))

    for sweep in range(SWEEPS):
        current = start if sweep == 0 else iterate
        halo_wait(sweep)

        def smooth_column(x, carry, sweep=sweep, current=current):
            for y in range(2):
                total = apply_fine(sweep, x, y)
                for z in range(2):
                    for parity in range(2):
                        at = z * B + parity * H
                        natural[y, z, every_second(parity), :] = total[at : at + H]
                res = [(rhs[x, y, z] - natural[y, z]).astype(BF16) for z in range(2)]
                delta = DAMPING * dot(smooth[2 * x + y], jnp.concatenate(res, axis=0))
                for z in range(2):
                    for parity in range(2):
                        at = z * B + parity * H
                        natural[y, z, every_second(parity), :] = delta[at : at + H]
                    new = current[x, y, z] + natural[y, z]
                    iterate[x, y, z] = new
                    padded[sweep + 1, x + 1, y + 1, pl.ds(z * B, B), :] = new.astype(BF16)
            return carry

        lax.fori_loop(0, size_x, smooth_column, 0)
        halo_start(sweep + 1)

    halo_wait(SWEEPS)

    def project_column(x, carry):
        for y in range(2):
            total = apply_fine(SWEEPS, x, y)
            res = []
            for z in range(2):
                for parity in range(2):
                    at = z * B + parity * H
                    side = rhs[x, y, z, every_second(parity), :]
                    res.append((side - total[at : at + H]).astype(BF16))
            projected[y, x] = lax.dot_general(
                transfer[2 * x + y],
                jnp.concatenate(res, axis=0),
                (((0,), (0,)), ((), ())),
                preferred_element_type=F32,
            )
        return carry

    lax.fori_loop(0, size_x, project_column, 0)

    def group_column(a, carry):
        for z in range(2):
            rows = pl.ds(z * B, B)
            total = (
                projected[0, inverse[z * size_x + a], rows, :]
                + projected[1, inverse[(2 + z) * size_x + a], rows, :]
            )
            csend[a, rows, :] = total.astype(BF16)
        return carry

    lax.fori_loop(0, size_x, group_column, 0)

    def to_coarse(r):
        other_l, other_d = ring(r)
        return pltpu.make_async_remote_copy(
            src_ref=csend.at[other_l],
            dst_ref=cres.at[depth, lateral],
            send_sem=to_send.at[r],
            recv_sem=to_recv.at[r],
            device_id=(track, other_l, other_d),
            device_id_type=MESH,
        )

    for r in range(1, group):
        to_coarse(r).start()
    cres[depth, lateral] = csend[lateral]
    partner.wait()
    for r in range(1, group):
        from_l, from_d = ring(group - r)
        pltpu.make_async_remote_copy(
            src_ref=csend.at[from_l],
            dst_ref=cres.at[from_d, from_l],
            send_sem=to_send.at[r],
            recv_sem=to_recv.at[r],
            device_id=(track, from_l, from_d),
            device_id_type=MESH,
        ).wait_recv()
    for r in range(1, group):
        to_coarse(r).wait_send()

    low = lanes_low(B)

    def first_pair(pair, carry):
        for z in range(2):
            rows = pl.ds(z * B, B)
            stack = [
                jnp.concatenate([cres[h, 2 * pair + k, rows, :] for h in range(2)], axis=1)
                for k in range(2)
            ]
            block = call[z, pair]
            zero = jnp.zeros_like(block)
            left = jnp.concatenate(
                [jnp.where(low, block, zero), jnp.where(low, zero, block)], axis=0
            )
            value = DAMPING * dot(left, jnp.concatenate(stack, axis=0))
            for k in range(2):
                for h in range(2):
                    for parity in range(2):
                        at = k * B + parity * H
                        first[z, h, 2 * pair + k, every_second(parity), :] = value[
                            at : at + H, h * LD : (h + 1) * LD
                        ]
                    cpad[1, h, 2 * pair + k + 1, rows, :] = first[z, h, 2 * pair + k].astype(BF16)
        return carry

    lax.fori_loop(0, size_l // 2, first_pair, 0)

    def side_copy(index):
        rows = pl.ds(1, size_l)
        return pltpu.make_async_remote_copy(
            src_ref=cpad.at[1, :, rows],
            dst_ref=cpad.at[2 - 2 * index, :, rows],
            send_sem=side_send.at[index],
            recv_sem=side_recv.at[index],
            device_id=sides[index][0],
            device_id_type=MESH,
        )

    for index in range(2):
        @pl.when(sides[index][1])
        def _(index=index):
            side_copy(index).start()
    for index in range(2):
        @pl.when(sides[1 - index][1])
        def _(index=index):
            side_copy(index).wait_recv()

        @pl.when(sides[index][1])
        def _(index=index):
            side_copy(index).wait_send()

    own_rows = pl.ds(pl.multiple_of(depth * B, B), B)

    def coarse_row(y, carry):
        pieces = [
            jnp.concatenate(
                [cpad[dx, h, pl.ds(y, 3)].reshape(3 * 128, LD) for h in range(2)], axis=1
            )
            for dx in range(3)
        ]
        pieces.append(jnp.concatenate([cpad[1, h, y + 1] for h in range(2)], axis=1))
        total = dot(coarse[y], jnp.concatenate(pieces, axis=0))
        remain = []
        for h in range(2):
            for parity in range(2):
                cnatural[h, every_second(parity), :] = total[
                    parity * H : (parity + 1) * H, h * LD : (h + 1) * LD
                ]
            remain.append((cres[h, y, own_rows, :].astype(F32) - cnatural[h]).astype(BF16))
        remain = jnp.concatenate(remain, axis=1)
        block = call[depth, y // 2]
        left = jnp.where(low == (lax.rem(y, 2) == 0), block, jnp.zeros_like(block))
        delta = DAMPING * dot(left, jnp.concatenate([remain, remain], axis=0))
        for h in range(2):
            for parity in range(2):
                cnatural[h, every_second(parity), :] = delta[
                    parity * H : (parity + 1) * H, h * LD : (h + 1) * LD
                ]
            csend_back[h, y] = (first[depth, h, y] + cnatural[h]).astype(BF16)
        return carry

    lax.fori_loop(0, size_l, coarse_row, 0)

    def to_fine(r):
        other_l, other_d = ring(r)
        return pltpu.make_async_remote_copy(
            src_ref=csend_back.at[other_d, other_l],
            dst_ref=corr.at[depth, lateral],
            send_sem=back_send.at[r],
            recv_sem=back_recv.at[r],
            device_id=(track, other_l, other_d),
            device_id_type=MESH,
        )

    for r in range(1, group):
        to_fine(r).start()
    corr[depth, lateral] = csend_back[depth, lateral]
    for r in range(1, group):
        from_l, from_d = ring(group - r)
        pltpu.make_async_remote_copy(
            src_ref=csend_back.at[from_d, from_l],
            dst_ref=corr.at[from_d, from_l],
            send_sem=back_send.at[r],
            recv_sem=back_recv.at[r],
            device_id=(track, from_l, from_d),
            device_id_type=MESH,
        ).wait_recv()
    for r in range(1, group):
        to_fine(r).wait_send()

    def final_column(x, carry):
        for y in range(2):
            parts = [corr[z, lax.rem(agg[x, y, z], size_x)] for z in range(2)]
            added = dot(transfer[2 * x + y], jnp.concatenate(parts, axis=0))
            for z in range(2):
                for parity in range(2):
                    at = z * B + parity * H
                    rows = every_second(parity)
                    out[x, y, z, rows, :] = iterate[x, y, z, rows, :] + added[at : at + H]
        return carry

    lax.fori_loop(0, size_x, final_column, 0)


def run_cycle(tracks, aggregate, inverse, rhs, start, fine, smooth, transfer, coarse, csmooth):
    size_x = rhs.shape[0]
    group = 2 * size_x
    smem = pl.BlockSpec(memory_space=pltpu.SMEM)
    vmem = pl.BlockSpec(memory_space=pltpu.VMEM)
    dma = pltpu.SemaphoreType.DMA
    return pl.pallas_call(
        functools.partial(cycle_kernel, tracks),
        in_specs=[smem] * 2 + [vmem] * 7,
        out_specs=vmem,
        out_shape=jax.ShapeDtypeStruct(rhs.shape, F32),
        scratch_shapes=[
            pltpu.VMEM((SWEEPS + 1, size_x + 2, 4, 128, LD), BF16),
            pltpu.VMEM(rhs.shape, F32),
            pltpu.VMEM((2, 2, B, LD), F32),
            pltpu.VMEM((2, size_x, 128, LD), F32),
            pltpu.VMEM((size_x, 128, LD), BF16),
            pltpu.VMEM((2, size_x, 128, LD), BF16),
            pltpu.VMEM((3, 2, size_x + 2, 128, LD), BF16),
            pltpu.VMEM((2, size_x // 2, B, 128), BF16),
            pltpu.VMEM((2, 2, size_x, B, LD), F32),
            pltpu.VMEM((2, size_x, B, LD), BF16),
            pltpu.VMEM((2, size_x, B, LD), BF16),
            pltpu.VMEM((2, B, LD), F32),
            dma((SWEEPS + 1, 8)), dma((SWEEPS + 1, 8)),
            dma((group,)), dma((group,)), dma((group,)), dma((group,)),
            dma((2,)), dma((2,)), dma, dma,
        ],
        compiler_params=pltpu.CompilerParams(
            collective_id=0, has_side_effects=True, vmem_limit_bytes=40 << 20
        ),
        name="cycle",
    )(aggregate, inverse, rhs, start, fine, smooth, transfer, coarse, csmooth)


def solution(mesh):
    tracks = mesh.shape["track"]

    def per_device(
        rhs, start, fine_blocks, fine_cols, fine_mass, fine_smoother, transfer, aggregate,
        coarse_blocks, coarse_cols, coarse_mass, coarse_smoother,
    ):
        fine, smooth, moved, coarse, csmooth, inverse = prepare(
            fine_blocks, fine_cols, fine_mass, fine_smoother, transfer, aggregate,
            coarse_blocks, coarse_cols, coarse_mass, coarse_smoother,
        )
        return run_cycle(
            tracks, aggregate, inverse, rhs, start, fine, smooth, moved, coarse, csmooth
        )

    in_specs = (
        P("track", "lateral", None, None, "depth"),
        P("track", "lateral", None, None, "depth"),
        P("track", "lateral", None, None, None),
        P("track", "lateral", None, None),
        P("track", "lateral", None, None),
        P("track", "lateral", None, None),
        P("track", "lateral", None, None),
        P("track", "lateral", None),
        P(("track", "lateral"), None, "depth", None, None),
        P(("track", "lateral"), None, "depth", None),
        P(("track", "lateral"), None, "depth", None),
        P(("track", "lateral"), None, "depth", None),
    )
    out_specs = P("track", "lateral", None, None, "depth")
    return jax.shard_map(
        per_device, mesh=mesh, in_specs=in_specs, out_specs=out_specs, check_vma=False
    )
```

```python
import functools

import jax
import jax.numpy as jnp
from jax import lax
from jax.experimental import pallas as pl
from jax.experimental.pallas import tpu as pltpu
from jax.sharding import PartitionSpec as P

SWEEPS = 2
DAMPING = 0.8
B = 64
H = B // 2
CODES = 27
LD = 128
WIDE = 10 * 128
F32 = jnp.float32
BF16 = jnp.bfloat16
MESH = pl.DeviceIdType.MESH
STEPS = [(0, -1), (0, 1), (-1, 0), (1, 0), (-1, -1), (-1, 1), (1, -1), (1, 1)]


def lanes_low(rows):
    return lax.broadcasted_iota(jnp.int32, (rows, 128), 1) < B


def half_swap(block):
    return jnp.concatenate([block[:, B:], block[:, :B]], axis=1)


def even_odd(low, first, second):
    return jnp.where(low, first, half_swap(second)), jnp.where(low, half_swap(first), second)


def fine_order(index):
    return index % 2 * B + index % B // 2 * 2 + index // B


def coarse_order(index):
    return index // B * B + index % H * 2 + index % B // H


def order_matrix(order):
    row = lax.broadcasted_iota(jnp.int32, (128, 128), 0)
    col = lax.broadcasted_iota(jnp.int32, (128, 128), 1)
    return (row == order(col)).astype(F32).astype(BF16)


def exact_dot(left, right):
    return dot(left, right).astype(BF16)


def prep_kernel(
    fcols, ccols, agg, fblk, fmass, fsm, tran, cblk, cmass, csm,
    fine, smooth, transfer, coarse, csmooth, inverse,
    spread, slots,
):
    step = pl.program_id(0)
    x = step // 2
    y = step % 2
    size_x = agg.shape[2]
    low = lanes_low(B)
    upper = lax.broadcasted_iota(jnp.int32, (B, 128), 0) % 2 == 0

    for layer in range(2):
        for k in range(CODES):
            slots[layer * CODES + fcols[x, y, layer, k]] = k

    def block(layer, code):
        return fblk[0, slots[layer * CODES + code]]

    for near in range(9):
        code = near * 3 + 1
        first = jnp.where(upper, block(0, code), block(1, code - 1))
        second = jnp.where(upper, block(0, code + 1), block(1, code))
        even, odd = even_odd(low, first, second)
        at = pl.ds(near * 128, 128)
        fine[0, pl.ds(0, B), at] = even
        fine[0, pl.ds(B, B), at] = odd
    row = lax.broadcasted_iota(jnp.int32, (128, 128), 0)
    col = lax.broadcasted_iota(jnp.int32, (128, 128), 1)
    mass = fmass[0, 0].astype(F32)
    mass = jnp.concatenate([mass[0:1], mass[1:2]], axis=1)
    diag = jnp.where(fine_order(row) == col, jnp.broadcast_to(mass, (128, 128)), 0.0)
    fine[0, :, pl.ds(9 * 128, 128)] = diag.astype(BF16)

    for source, target, order in ((fsm, smooth, fine_order), (tran, transfer, coarse_order)):
        whole = source[0]
        zero = jnp.zeros_like(whole)
        even, odd = even_odd(low, jnp.where(upper, whole, zero), jnp.where(upper, zero, whole))
        both = jnp.concatenate([even, odd], axis=0)
        target[0] = exact_dot(both, order_matrix(order))

    @pl.when(step == 0)
    def _():
        for slot in range(CODES):
            spread[slot] = cblk[slot].astype(F32)
        spread[CODES] = csm[...].astype(F32)
        for pair in range(size_x // 2):
            parts = [spread[CODES, pl.ds(2 * pair + k, H, stride=size_x), :] for k in range(2)]
            even, odd = even_odd(low[:H], *parts)
            both = jnp.concatenate([even, odd], axis=0).astype(BF16)
            csmooth[pair] = exact_dot(both, order_matrix(coarse_order))
        for side in range(2):
            for layer in range(2):
                for place in range(size_x):
                    at = (side * 2 + layer) * size_x
                    inverse[at + lax.rem(agg[side, layer, place], size_x)] = place

    @pl.when(y == 0)
    def _():
        depth = lax.axis_index("depth")
        for k in range(CODES):
            slots[ccols[0, x, 0, k]] = k
        for near in range(9):
            parts = []
            for z in range(2):
                slot = slots[near * 3 + 1 + z - depth]
                parts.append(spread[slot, pl.ds(x, H, stride=size_x), :])
            even, odd = even_odd(low[:H], *parts)
            at = pl.ds(near * 128, 128)
            coarse[0, pl.ds(0, H), at] = even.astype(BF16)
            coarse[0, pl.ds(H, H), at] = odd.astype(BF16)
        mass = cmass[pl.ds(x, 1), :]
        mass = jnp.broadcast_to(jnp.concatenate([mass, mass], axis=1), (B, 128))
        wanted = coarse_order(row[:B]) + depth * B
        coarse[0, :, pl.ds(9 * 128, 128)] = jnp.where(wanted == col[:B], mass, 0.0).astype(BF16)


def prepare(fine_blocks, fine_cols, fine_mass, fine_smoother, transfer, aggregate,
            coarse_blocks, coarse_cols, coarse_mass, coarse_smoother):
    size_x = fine_blocks.shape[0]
    count = 2 * size_x
    tiles = B * B // 128
    fine_blocks = fine_blocks.reshape(size_x, 2, 2, CODES, tiles, 128)
    fine_blocks = jnp.transpose(fine_blocks, (0, 1, 3, 4, 2, 5)).reshape(count, CODES, B, 128)
    pair = []
    for array in (fine_smoother, transfer):
        array = jnp.transpose(array.reshape(size_x, 2, 2, tiles, 128), (0, 1, 3, 2, 4))
        pair.append(array.reshape(count, B, 128))
    coarse_blocks = coarse_blocks.reshape(size_x, CODES, tiles, 128)
    coarse_blocks = jnp.transpose(coarse_blocks, (1, 2, 0, 3)).reshape(CODES, tiles * size_x, 128)
    coarse_smoother = jnp.transpose(coarse_smoother.reshape(size_x, tiles, 128), (1, 0, 2))
    coarse_smoother = coarse_smoother.reshape(tiles * size_x, 128)
    smem = pl.BlockSpec(memory_space=pltpu.SMEM)
    vmem = pl.BlockSpec(memory_space=pltpu.VMEM)

    def per_step(*rest):
        return pl.BlockSpec((1,) + rest, lambda i: (i,) + (0,) * len(rest))

    return pl.pallas_call(
        prep_kernel,
        grid=(count,),
        in_specs=[
            smem, smem, smem,
            per_step(CODES, B, 128),
            pl.BlockSpec((1, 1, 2, B), lambda i: (i // 2, i % 2, 0, 0)),
            per_step(B, 128), per_step(B, 128),
            vmem, vmem, vmem,
        ],
        out_specs=[
            per_step(128, WIDE), per_step(128, 128), per_step(128, 128),
            pl.BlockSpec((1, B, WIDE), lambda i: (i // 2, 0, 0)),
            pl.BlockSpec((size_x // 2, B, 128), lambda i: (0, 0, 0)),
            smem,
        ],
        out_shape=[
            jax.ShapeDtypeStruct((count, 128, WIDE), BF16),
            jax.ShapeDtypeStruct((count, 128, 128), BF16),
            jax.ShapeDtypeStruct((count, 128, 128), BF16),
            jax.ShapeDtypeStruct((size_x, B, WIDE), BF16),
            jax.ShapeDtypeStruct((size_x // 2, B, 128), BF16),
            jax.ShapeDtypeStruct((4 * size_x,), jnp.int32),
        ],
        scratch_shapes=[
            pltpu.VMEM((CODES + 1, tiles * size_x, 128), F32),
            pltpu.SMEM((2 * CODES,), jnp.int32),
        ],
        compiler_params=pltpu.CompilerParams(vmem_limit_bytes=32 << 20),
        name="prepare",
    )(fine_cols, coarse_cols, aggregate, fine_blocks, fine_mass, *pair, coarse_blocks,
      coarse_mass.reshape(size_x, B).astype(F32), coarse_smoother)


def dot(left, right):
    return jnp.dot(left, right, preferred_element_type=F32)


def every_second(parity):
    return pl.ds(parity, H, stride=2)


def cycle_kernel(
    tracks, agg, inverse, rhs, start, fine, smooth, transfer, coarse, csmooth,
    out,
    padded, forces, iterate, projected, csend, cres, cpad, call, first, csend_back, corr,
    halo_send, halo_recv, to_send, to_recv, back_send, back_recv, side_send, side_recv,
    ss_send, ss_recv,
):
    size_x = rhs.shape[0]
    size_l = size_x
    track = lax.axis_index("track")
    lateral = lax.axis_index("lateral")
    depth = lax.axis_index("depth")
    group = 2 * size_l
    me = lateral * 2 + depth

    def exists(dt, dl):
        ok = None
        for step, at, count in ((dt, track, tracks), (dl, lateral, size_l)):
            if step:
                here = (at > 0) if step < 0 else (at < count - 1)
                ok = here if ok is None else jnp.logical_and(ok, here)
        return ok

    def ring(r):
        other = lax.rem(me + r, group)
        return other // 2, lax.rem(other, 2)

    last = size_l - 1
    before = (track - (lateral == 0).astype(jnp.int32), lax.rem(lateral + last, size_l), depth)
    after = (track + (lateral == last).astype(jnp.int32), lax.rem(lateral + 1, size_l), depth)
    sides = (
        (before, jnp.logical_or(track > 0, lateral > 0)),
        (after, jnp.logical_or(track < tracks - 1, lateral < last)),
    )

    for sweep in range(SWEEPS + 1):
        for place in (0, size_x + 1):
            padded[sweep, place] = jnp.zeros_like(padded[sweep, place])
        for place in (0, 3):
            padded[sweep, :, place] = jnp.zeros_like(padded[sweep, :, place])
    for place in (0, 2):
        cpad[place] = jnp.zeros_like(cpad[place])
    for place in (0, size_l + 1):
        cpad[1, :, place] = jnp.zeros_like(cpad[1, :, place])

    barrier = pltpu.get_barrier_semaphore()
    for r in range(1, group):
        other_l, other_d = ring(r)
        pl.semaphore_signal(barrier, inc=1, device_id=(track, other_l, other_d), device_id_type=MESH)
    expected = group - 1
    for dt, dl in STEPS:
        if dt:
            ok = exists(dt, dl)

            @pl.when(ok)
            def _(dt=dt, dl=dl):
                pl.semaphore_signal(
                    barrier, inc=1, device_id=(track + dt, lateral + dl, depth), device_id_type=MESH
                )

            expected = expected + ok.astype(jnp.int32)
    for (device, ok), at_end in zip(sides, (lateral == 0, lateral == last)):
        crossing = jnp.logical_and(ok, at_end)

        @pl.when(crossing)
        def _(device=device):
            pl.semaphore_signal(barrier, inc=1, device_id=device, device_id_type=MESH)

        expected = expected + crossing.astype(jnp.int32)

    def round_start(x, carry):
        for y in range(2):
            for z in range(2):
                padded[0, x + 1, y + 1, pl.ds(z * B, B), :] = start[x, y, z].astype(BF16)
        return carry

    def reorder(x, carry):
        for y in range(2):
            for z in range(2):
                for parity in range(2):
                    rows = every_second(parity * B + z)
                    for source, target in ((rhs, forces), (start, iterate)):
                        target[x, y, rows, :] = source[x, y, z, every_second(parity), :]
        return carry

    lax.fori_loop(0, size_x, round_start, 0)
    pl.semaphore_wait(barrier, expected)

    def halo_copy(sweep, index):
        dt, dl = STEPS[index]
        src_x, dst_x = {0: (pl.ds(1, size_x),) * 2, -1: (1, size_x + 1), 1: (size_x, 0)}[dt]
        src_y, dst_y = {0: (pl.ds(1, 2),) * 2, -1: (1, 3), 1: (2, 0)}[dl]
        return pltpu.make_async_remote_copy(
            src_ref=padded.at[sweep, src_x, src_y],
            dst_ref=padded.at[sweep, dst_x, dst_y],
            send_sem=halo_send.at[sweep, index],
            recv_sem=halo_recv.at[sweep, index],
            device_id=(track + dt, lateral + dl, depth),
            device_id_type=MESH,
        )

    def halo_start(sweep):
        for index, (dt, dl) in enumerate(STEPS):
            @pl.when(exists(dt, dl))
            def _(index=index):
                halo_copy(sweep, index).start()

    def halo_wait(sweep):
        for index, (dt, dl) in enumerate(STEPS):
            @pl.when(exists(-dt, -dl))
            def _(index=index):
                halo_copy(sweep, index).wait_recv()

            @pl.when(exists(dt, dl))
            def _(index=index):
                halo_copy(sweep, index).wait_send()

    halo_start(0)
    call[depth] = csmooth[...]
    partner = pltpu.make_async_remote_copy(
        src_ref=call.at[depth],
        dst_ref=call.at[depth],
        send_sem=ss_send,
        recv_sem=ss_recv,
        device_id=(track, lateral, 1 - depth),
        device_id_type=MESH,
    )
    partner.start()

    def apply_fine(sweep, x, y):
        pieces = [
            padded[sweep, x + dx, pl.ds(y, 3)].reshape(3 * 128, LD) for dx in range(3)
        ]
        pieces.append(padded[sweep, x + 1, y + 1])
        return dot(fine[2 * x + y], jnp.concatenate(pieces, axis=0))

    lax.fori_loop(0, size_x, reorder, 0)
    swap = order_matrix(fine_order)

    for sweep in range(SWEEPS):
        halo_wait(sweep)

        def smooth_column(x, carry, sweep=sweep):
            totals = [apply_fine(sweep, x, y) for y in range(2)]
            res = [(forces[x, y] - totals[y]).astype(BF16) for y in range(2)]
            steps = [DAMPING * dot(smooth[2 * x + y], res[y]) for y in range(2)]
            for y in range(2):
                new = iterate[x, y] + steps[y]
                iterate[x, y] = new
                padded[sweep + 1, x + 1, y + 1] = exact_dot(swap, new.astype(BF16))
            return carry

        lax.fori_loop(0, size_x, smooth_column, 0)
        halo_start(sweep + 1)

    halo_wait(SWEEPS)

    def project_column(x, carry):
        for y in range(2):
            res = (forces[x, y] - apply_fine(SWEEPS, x, y)).astype(BF16)
            projected[y, x] = lax.dot_general(
                transfer[2 * x + y], res, (((0,), (0,)), ((), ())), preferred_element_type=F32
            )
        return carry

    lax.fori_loop(0, size_x, project_column, 0)

    def group_column(a, carry):
        for z in range(2):
            rows = pl.ds(z * B, B)
            total = (
                projected[0, inverse[z * size_x + a], rows, :]
                + projected[1, inverse[(2 + z) * size_x + a], rows, :]
            )
            csend[a, rows, :] = total.astype(BF16)
        return carry

    lax.fori_loop(0, size_x, group_column, 0)

    def to_coarse(r):
        other_l, other_d = ring(r)
        return pltpu.make_async_remote_copy(
            src_ref=csend.at[other_l],
            dst_ref=cres.at[depth, lateral],
            send_sem=to_send.at[r],
            recv_sem=to_recv.at[r],
            device_id=(track, other_l, other_d),
            device_id_type=MESH,
        )

    for r in range(1, group):
        to_coarse(r).start()
    cres[depth, lateral] = csend[lateral]
    partner.wait()
    for r in range(1, group):
        from_l, from_d = ring(group - r)
        pltpu.make_async_remote_copy(
            src_ref=csend.at[from_l],
            dst_ref=cres.at[from_d, from_l],
            send_sem=to_send.at[r],
            recv_sem=to_recv.at[r],
            device_id=(track, from_l, from_d),
            device_id_type=MESH,
        ).wait_recv()
    for r in range(1, group):
        to_coarse(r).wait_send()

    low = lanes_low(B)
    order = order_matrix(coarse_order)

    def first_pair(pair, carry):
        for z in range(2):
            rows = pl.ds(z * B, B)
            stack = [
                jnp.concatenate([cres[h, 2 * pair + k, rows, :] for h in range(2)], axis=1)
                for k in range(2)
            ]
            block = call[z, pair]
            zero = jnp.zeros_like(block)
            left = jnp.concatenate(
                [jnp.where(low, block, zero), jnp.where(low, zero, block)], axis=0
            )
            value = DAMPING * dot(left, jnp.concatenate(stack, axis=0))
            plain = exact_dot(order, value.astype(BF16))
            for k in range(2):
                for h in range(2):
                    lanes = slice(h * LD, (h + 1) * LD)
                    first[z, h, 2 * pair + k] = value[k * B : (k + 1) * B, lanes]
                    cpad[1, h, 2 * pair + k + 1, rows, :] = plain[k * B : (k + 1) * B, lanes]
        return carry

    lax.fori_loop(0, size_l // 2, first_pair, 0)

    def side_copy(index):
        rows = pl.ds(1, size_l)
        return pltpu.make_async_remote_copy(
            src_ref=cpad.at[1, :, rows],
            dst_ref=cpad.at[2 - 2 * index, :, rows],
            send_sem=side_send.at[index],
            recv_sem=side_recv.at[index],
            device_id=sides[index][0],
            device_id_type=MESH,
        )

    for index in range(2):
        @pl.when(sides[index][1])
        def _(index=index):
            side_copy(index).start()
    for index in range(2):
        @pl.when(sides[1 - index][1])
        def _(index=index):
            side_copy(index).wait_recv()

        @pl.when(sides[index][1])
        def _(index=index):
            side_copy(index).wait_send()

    own_rows = pl.ds(pl.multiple_of(depth * B, B), B)

    def coarse_row(y, carry):
        pieces = [
            jnp.concatenate(
                [cpad[dx, h, pl.ds(y, 3)].reshape(3 * 128, LD) for h in range(2)], axis=1
            )
            for dx in range(3)
        ]
        pieces.append(jnp.concatenate([cpad[1, h, y + 1] for h in range(2)], axis=1))
        total = dot(coarse[y], jnp.concatenate(pieces, axis=0))
        held = jnp.concatenate([cres[h, y, own_rows, :] for h in range(2)], axis=1)
        remain = (held.astype(F32) - total).astype(BF16)
        block = call[depth, y // 2]
        left = jnp.where(low == (lax.rem(y, 2) == 0), block, jnp.zeros_like(block))
        delta = DAMPING * dot(left, jnp.concatenate([remain, remain], axis=0))
        for h in range(2):
            new = first[depth, h, y] + delta[:, h * LD : (h + 1) * LD]
            csend_back[h, y] = new.astype(BF16)
        return carry

    lax.fori_loop(0, size_l, coarse_row, 0)

    def to_fine(r):
        other_l, other_d = ring(r)
        return pltpu.make_async_remote_copy(
            src_ref=csend_back.at[other_d, other_l],
            dst_ref=corr.at[depth, lateral],
            send_sem=back_send.at[r],
            recv_sem=back_recv.at[r],
            device_id=(track, other_l, other_d),
            device_id_type=MESH,
        )

    for r in range(1, group):
        to_fine(r).start()
    corr[depth, lateral] = csend_back[depth, lateral]
    for r in range(1, group):
        from_l, from_d = ring(group - r)
        pltpu.make_async_remote_copy(
            src_ref=csend_back.at[from_d, from_l],
            dst_ref=corr.at[from_d, from_l],
            send_sem=back_send.at[r],
            recv_sem=back_recv.at[r],
            device_id=(track, from_l, from_d),
            device_id_type=MESH,
        ).wait_recv()
    for r in range(1, group):
        to_fine(r).wait_send()

    def final_column(x, carry):
        for y in range(2):
            parts = [corr[z, lax.rem(agg[y, z, x], size_x)] for z in range(2)]
            iterate[x, y] += dot(transfer[2 * x + y], jnp.concatenate(parts, axis=0))
            for z in range(2):
                for parity in range(2):
                    rows = every_second(parity * B + z)
                    out[x, y, z, every_second(parity), :] = iterate[x, y, rows, :]
        return carry

    lax.fori_loop(0, size_x, final_column, 0)


def run_cycle(tracks, aggregate, inverse, rhs, start, fine, smooth, transfer, coarse, csmooth):
    size_x = rhs.shape[0]
    group = 2 * size_x
    smem = pl.BlockSpec(memory_space=pltpu.SMEM)
    vmem = pl.BlockSpec(memory_space=pltpu.VMEM)
    dma = pltpu.SemaphoreType.DMA
    return pl.pallas_call(
        functools.partial(cycle_kernel, tracks),
        in_specs=[smem] * 2 + [vmem] * 7,
        out_specs=vmem,
        out_shape=jax.ShapeDtypeStruct(rhs.shape, F32),
        scratch_shapes=[
            pltpu.VMEM((SWEEPS + 1, size_x + 2, 4, 128, LD), BF16),
            pltpu.VMEM((size_x, 2, 128, LD), F32),
            pltpu.VMEM((size_x, 2, 128, LD), F32),
            pltpu.VMEM((2, size_x, 128, LD), F32),
            pltpu.VMEM((size_x, 128, LD), BF16),
            pltpu.VMEM((2, size_x, 128, LD), BF16),
            pltpu.VMEM((3, 2, size_x + 2, 128, LD), BF16),
            pltpu.VMEM((2, size_x // 2, B, 128), BF16),
            pltpu.VMEM((2, 2, size_x, B, LD), F32),
            pltpu.VMEM((2, size_x, B, LD), BF16),
            pltpu.VMEM((2, size_x, B, LD), BF16),
            dma((SWEEPS + 1, 8)), dma((SWEEPS + 1, 8)),
            dma((group,)), dma((group,)), dma((group,)), dma((group,)),
            dma((2,)), dma((2,)), dma, dma,
        ],
        compiler_params=pltpu.CompilerParams(
            collective_id=0, has_side_effects=True, vmem_limit_bytes=40 << 20
        ),
        name="cycle",
    )(aggregate, inverse, rhs, start, fine, smooth, transfer, coarse, csmooth)


def solution(mesh):
    tracks = mesh.shape["track"]

    def per_device(
        rhs, start, fine_blocks, fine_cols, fine_mass, fine_smoother, transfer, aggregate,
        coarse_blocks, coarse_cols, coarse_mass, coarse_smoother,
    ):
        aggregate = jnp.transpose(aggregate, (1, 2, 0))
        fine, smooth, moved, coarse, csmooth, inverse = prepare(
            fine_blocks, fine_cols, fine_mass, fine_smoother, transfer, aggregate,
            coarse_blocks, coarse_cols, coarse_mass, coarse_smoother,
        )
        return run_cycle(
            tracks, aggregate, inverse, rhs, start, fine, smooth, moved, coarse, csmooth
        )

    in_specs = (
        P("track", "lateral", None, None, "depth"),
        P("track", "lateral", None, None, "depth"),
        P("track", "lateral", None, None, None),
        P("track", "lateral", None, None),
        P("track", "lateral", None, None),
        P("track", "lateral", None, None),
        P("track", "lateral", None, None),
        P("track", "lateral", None),
        P(("track", "lateral"), None, "depth", None, None),
        P(("track", "lateral"), None, "depth", None),
        P(("track", "lateral"), None, "depth", None),
        P(("track", "lateral"), None, "depth", None),
    )
    out_specs = P("track", "lateral", None, None, "depth")
    return jax.shard_map(
        per_device, mesh=mesh, in_specs=in_specs, out_specs=out_specs, check_vma=False
    )
```

```python
import functools

import jax
import jax.numpy as jnp
from jax import lax
from jax.experimental import pallas as pl
from jax.experimental.pallas import tpu as pltpu
from jax.sharding import PartitionSpec as P

SWEEPS = 2
DAMPING = 0.8
B = 64
H = B // 2
CODES = 27
LD = 128
WIDE = 10 * 128
F32 = jnp.float32
BF16 = jnp.bfloat16
MESH = pl.DeviceIdType.MESH


def lanes_low(rows):
    return lax.broadcasted_iota(jnp.int32, (rows, 128), 1) < B


def half_swap(block):
    return jnp.concatenate([block[:, B:], block[:, :B]], axis=1)


def even_odd(low, first, second):
    return jnp.where(low, first, half_swap(second)), jnp.where(low, half_swap(first), second)


def fine_order(index):
    return index % 2 * B + index % B // 2 * 2 + index // B


def coarse_order(index):
    return index // B * B + index % H * 2 + index % B // H


def order_matrix(order):
    row = lax.broadcasted_iota(jnp.int32, (128, 128), 0)
    col = lax.broadcasted_iota(jnp.int32, (128, 128), 1)
    return (row == order(col)).astype(F32).astype(BF16)


def exact_dot(left, right):
    return dot(left, right).astype(BF16)


def dot(left, right):
    return jnp.dot(left, right, preferred_element_type=F32)


def every_second(parity):
    return pl.ds(parity, H, stride=2)


def inverse_rows(lists, count):
    rows = lists.shape[0]
    lane = lax.broadcasted_iota(jnp.int32, (rows, 128), 1)
    found = jnp.zeros((rows, 128), jnp.int32)
    for k in range(count):
        found = jnp.where(lists[:, k : k + 1] == lane, k, found)
    return found


def cycle_kernel(
    tracks,
    rhs_hbm, start_hbm, fblk_hbm, fcols_hbm, fmass_hbm, fsm_hbm, tran_hbm, agg_hbm,
    cblk_hbm, ccols_hbm, cmass_hbm, csm_hbm,
    out,
    rhs, start, fblk, fcols, fmass, fsm, tran, agg, cblk, ccols, cmass, csm,
    rows_table, table, fine, smooth, transfer, coarse, spread,
    padded, forces, iterate, projected, csend, cres, cpad, call, first, csend_back, corr,
    load_sem, block_sem, table_sem,
    bulk_send, bulk_recv, lat_send, lat_recv, track_send, track_recv,
    to_send, to_recv, back_send, back_recv, side_send, side_recv, ss_send, ss_recv,
):
    size_x = rhs.shape[0]
    size_l = size_x
    count = 2 * size_x
    group = 2 * size_l
    last = size_x - 1
    track = lax.axis_index("track")
    lateral = lax.axis_index("lateral")
    depth = lax.axis_index("depth")
    me = lateral * 2 + depth

    small = [
        (start_hbm, start), (fcols_hbm, fcols), (ccols_hbm, ccols), (agg_hbm, agg),
        (fmass_hbm, fmass), (fsm_hbm, fsm), (tran_hbm, tran), (rhs_hbm, rhs),
        (csm_hbm, csm), (cmass_hbm, cmass), (cblk_hbm, cblk),
    ]
    loads = [
        pltpu.make_async_copy(source, target, load_sem.at[k])
        for k, (source, target) in enumerate(small)
    ]

    def block_load(i):
        return pltpu.make_async_copy(fblk_hbm.at[i], fblk.at[i], block_sem.at[i])

    for load in loads[:8]:
        load.start()

    def start_block(i, carry):
        block_load(i).start()
        return carry

    lax.fori_loop(0, count, start_block, 0)
    for load in loads[8:]:
        load.start()

    def exists(dt, dl):
        ok = None
        for step, at, ends in ((dt, track, tracks), (dl, lateral, size_l)):
            if step:
                here = (at > 0) if step < 0 else (at < ends - 1)
                ok = here if ok is None else jnp.logical_and(ok, here)
        return ok

    before = (track - (lateral == 0).astype(jnp.int32), lax.rem(lateral + last, size_l), depth)
    after = (track + (lateral == last).astype(jnp.int32), lax.rem(lateral + 1, size_l), depth)
    sides = (
        (before, jnp.logical_or(track > 0, lateral > 0)),
        (after, jnp.logical_or(track < tracks - 1, lateral < last)),
    )

    for sweep in range(SWEEPS + 1):
        for place in (0, size_x + 1):
            padded[sweep, place] = jnp.zeros_like(padded[sweep, place])
        for place in (0, 3):
            padded[sweep, :, place] = jnp.zeros_like(padded[sweep, :, place])
    for place in (0, 2):
        cpad[place] = jnp.zeros_like(cpad[place])
    for place in (0, size_l + 1):
        cpad[1, :, place] = jnp.zeros_like(cpad[1, :, place])

    barrier = pltpu.get_barrier_semaphore()
    for r in range(1, group):
        other = lax.rem(me + r, group)
        pl.semaphore_signal(
            barrier, inc=1, device_id=(track, other // 2, lax.rem(other, 2)), device_id_type=MESH
        )
    expected = group - 1
    for dt in (-1, 1):
        for dl in (-1, 0, 1):
            ok = exists(dt, dl)

            @pl.when(ok)
            def _(dt=dt, dl=dl):
                pl.semaphore_signal(
                    barrier, inc=1, device_id=(track + dt, lateral + dl, depth), device_id_type=MESH
                )

            expected = expected + ok.astype(jnp.int32)
    for (device, ok), at_end in zip(sides, (lateral == 0, lateral == last)):
        crossing = jnp.logical_and(ok, at_end)

        @pl.when(crossing)
        def _(device=device):
            pl.semaphore_signal(barrier, inc=1, device_id=device, device_id_type=MESH)

        expected = expected + crossing.astype(jnp.int32)

    def round_start(x, carry):
        for y in range(2):
            for z in range(2):
                padded[0, x + 1, y + 1, pl.ds(z * B, B), :] = start[x, y, z].astype(BF16)
        return carry

    loads[0].wait()
    lax.fori_loop(0, size_x, round_start, 0)
    pl.semaphore_wait(barrier, expected)

    def lateral_copy(sweep, x, side):
        if sweep == 0:
            columns, sems = pl.ds(1, size_x), (bulk_send.at[side], bulk_recv.at[side])
        else:
            sems = (lat_send.at[sweep - 1, side, x], lat_recv.at[sweep - 1, side, x])
            columns = x + 1
        return pltpu.make_async_remote_copy(
            src_ref=padded.at[sweep, columns, 1 + side],
            dst_ref=padded.at[sweep, columns, 3 - 3 * side],
            send_sem=sems[0],
            recv_sem=sems[1],
            device_id=(track, lateral + 2 * side - 1, depth),
            device_id_type=MESH,
        )

    def track_copy(sweep, side, dl):
        src_y, dst_y = {0: (pl.ds(1, 2),) * 2, -1: (1, 3), 1: (2, 0)}[dl]
        return pltpu.make_async_remote_copy(
            src_ref=padded.at[sweep, size_x if side else 1, src_y],
            dst_ref=padded.at[sweep, 0 if side else size_x + 1, dst_y],
            send_sem=track_send.at[sweep, side, dl + 1],
            recv_sem=track_recv.at[sweep, side, dl + 1],
            device_id=(track + 2 * side - 1, lateral + dl, depth),
            device_id_type=MESH,
        )

    def lateral_do(action, sweep, x):
        for side in range(2):
            step = 2 * side - 1

            @pl.when(exists(0, -step if action == "wait_recv" else step))
            def _(side=side):
                getattr(lateral_copy(sweep, x, side), action)()

    def track_do(action, sweep, side):
        step = 2 * side - 1
        for dl in (0, -1, 1):
            here = (-step, -dl) if action == "wait_recv" else (step, dl)

            @pl.when(exists(*here))
            def _(dl=dl):
                getattr(track_copy(sweep, side, dl), action)()

    lateral_do("start", 0, 0)
    for side in range(2):
        track_do("start", 0, side)

    for load in loads[1:4]:
        load.wait()
    rows_table[pl.ds(0, 4 * size_x), :] = inverse_rows(fcols[...], CODES)
    rows_table[pl.ds(4 * size_x, size_x), :] = inverse_rows(ccols[...], CODES)
    groups = lax.rem(agg[...], size_x)
    rows_table[pl.ds(5 * size_x, 4), :] = inverse_rows(groups, size_x)
    rows_table[pl.ds(5 * size_x + 4, 4), pl.ds(0, size_x)] = groups
    fill = pltpu.make_async_copy(rows_table, table, table_sem)
    fill.start()
    for load in loads[4:9]:
        load.wait()

    def reorder(x, carry):
        for y in range(2):
            for z in range(2):
                for parity in range(2):
                    rows = every_second(parity * B + z)
                    for source, target in ((rhs, forces), (start, iterate)):
                        target[x, y, rows, :] = source[x, y, z, every_second(parity), :]
        return carry

    lax.fori_loop(0, size_x, reorder, 0)
    swap = order_matrix(fine_order)
    order = order_matrix(coarse_order)
    low = lanes_low(B)
    upper = lax.broadcasted_iota(jnp.int32, (B, 128), 0) % 2 == 0
    row = lax.broadcasted_iota(jnp.int32, (128, 128), 0)
    col = lax.broadcasted_iota(jnp.int32, (128, 128), 1)

    spread[CODES] = csm[...].astype(F32)
    for pair in range(size_x // 2):
        parts = [spread[CODES, pl.ds(2 * pair + k, H, stride=size_x), :] for k in range(2)]
        even, odd = even_odd(low[:H], *parts)
        both = jnp.concatenate([even, odd], axis=0).astype(BF16)
        call[depth, pair] = exact_dot(both, order)
    partner = pltpu.make_async_remote_copy(
        src_ref=call.at[depth],
        dst_ref=call.at[depth],
        send_sem=ss_send,
        recv_sem=ss_recv,
        device_id=(track, lateral, 1 - depth),
        device_id_type=MESH,
    )
    partner.start()
    fill.wait()

    def wait_block(i, carry):
        block_load(i).wait()
        return carry

    lax.fori_loop(0, count, wait_block, 0)

    def sort_fine(i, carry):
        def block(layer, code):
            return fblk[i, table[2 * i + layer, code]]

        for near in range(9):
            code = near * 3 + 1
            one = jnp.where(upper, block(0, code), block(1, code - 1))
            two = jnp.where(upper, block(0, code + 1), block(1, code))
            even, odd = even_odd(low, one, two)
            at = pl.ds(near * 128, 128)
            fine[i, pl.ds(0, B), at] = even
            fine[i, pl.ds(B, B), at] = odd
        mass = fmass[i // 2, lax.rem(i, 2)].astype(F32)
        mass = jnp.concatenate([mass[0:1], mass[1:2]], axis=1)
        diag = jnp.where(fine_order(row) == col, jnp.broadcast_to(mass, (128, 128)), 0.0)
        fine[i, :, pl.ds(9 * 128, 128)] = diag.astype(BF16)
        for source, target, reordering in ((fsm, smooth, swap), (tran, transfer, order)):
            whole = source[i]
            zero = jnp.zeros_like(whole)
            even, odd = even_odd(low, jnp.where(upper, whole, zero), jnp.where(upper, zero, whole))
            target[i] = exact_dot(jnp.concatenate([even, odd], axis=0), reordering)
        return carry

    lax.fori_loop(0, count, sort_fine, 0)
    lateral_do("wait_recv", 0, 0)
    for side in range(2):
        track_do("wait_recv", 0, side)

    def apply_fine(sweep, x, y):
        pieces = [
            padded[sweep, x + dx, pl.ds(y, 3)].reshape(3 * 128, LD) for dx in range(3)
        ]
        pieces.append(padded[sweep, x + 1, y + 1])
        return dot(fine[2 * x + y], jnp.concatenate(pieces, axis=0))

    def smooth_column(sweep, x):
        totals = [apply_fine(sweep, x, y) for y in range(2)]
        res = [(forces[x, y] - totals[y]).astype(BF16) for y in range(2)]
        steps = [DAMPING * dot(smooth[2 * x + y], res[y]) for y in range(2)]
        for y in range(2):
            new = iterate[x, y] + steps[y]
            iterate[x, y] = new
            padded[sweep + 1, x + 1, y + 1] = exact_dot(swap, new.astype(BF16))
        lateral_do("start", sweep + 1, x)

        @pl.when(x == 0)
        def _():
            track_do("start", sweep + 1, 0)

        @pl.when(x == last)
        def _():
            track_do("start", sweep + 1, 1)

    def outer_first(i, carry):
        x = i - 1 + (i == 0).astype(jnp.int32) + (i == 1).astype(jnp.int32) * last
        smooth_column(0, x)
        return carry

    lax.fori_loop(0, size_x, outer_first, 0)

    def in_order(x, carry):
        @pl.when(x == 0)
        def _():
            lateral_do("wait_recv", 1, 0)
            track_do("wait_recv", 1, 1)

        @pl.when(x < last)
        def _():
            lateral_do("wait_recv", 1, x + 1)

        @pl.when(x == last)
        def _():
            track_do("wait_recv", 1, 0)

        smooth_column(1, x)
        return carry

    lax.fori_loop(0, size_x, in_order, 0)

    def project_column(i, carry):
        x = lax.rem(i + 1, size_x)

        @pl.when(i == 0)
        def _():
            lateral_do("wait_recv", 2, 0)
            lateral_do("wait_recv", 2, 1)

        @pl.when(jnp.logical_and(x > 0, x < last))
        def _():
            lateral_do("wait_recv", 2, x + 1)

        @pl.when(x == last)
        def _():
            track_do("wait_recv", 2, 0)

        @pl.when(x == 0)
        def _():
            track_do("wait_recv", 2, 1)

        for y in range(2):
            res = (forces[x, y] - apply_fine(SWEEPS, x, y)).astype(BF16)
            projected[y, x] = lax.dot_general(
                transfer[2 * x + y], res, (((0,), (0,)), ((), ())), preferred_element_type=F32
            )
        return carry

    lax.fori_loop(0, size_x, project_column, 0)

    def to_coarse(other_l, other_d):
        r = lax.rem(other_l * 2 + other_d - me + group, group)
        return r, pltpu.make_async_remote_copy(
            src_ref=csend.at[other_l],
            dst_ref=cres.at[depth, lateral],
            send_sem=to_send.at[r],
            recv_sem=to_recv.at[r],
            device_id=(track, other_l, other_d),
            device_id_type=MESH,
        )

    def group_column(a, carry):
        for z in range(2):
            rows = pl.ds(z * B, B)
            total = (
                projected[0, table[5 * size_x + z, a], rows, :]
                + projected[1, table[5 * size_x + 2 + z, a], rows, :]
            )
            csend[a, rows, :] = total.astype(BF16)
        for other_d in range(2):
            r, copy = to_coarse(a, other_d)

            @pl.when(r != 0)
            def _(copy=copy):
                copy.start()
        return carry

    lax.fori_loop(0, size_x, group_column, 0)
    cres[depth, lateral] = csend[lateral]

    for load in loads[9:]:
        load.wait()

    def widen(slot, carry):
        spread[slot] = cblk[slot].astype(F32)
        return carry

    lax.fori_loop(0, CODES, widen, 0)

    def sort_coarse(y, carry):
        for near in range(9):
            parts = []
            for z in range(2):
                slot = table[4 * size_x + y, near * 3 + 1 + z - depth]
                parts.append(spread[slot, pl.ds(y, H, stride=size_x), :])
            even, odd = even_odd(low[:H], *parts)
            at = pl.ds(near * 128, 128)
            coarse[y, pl.ds(0, H), at] = even.astype(BF16)
            coarse[y, pl.ds(H, H), at] = odd.astype(BF16)
        chosen = lax.broadcasted_iota(jnp.int32, (size_x, B), 0) == y
        mass = jnp.where(chosen, cmass[...].astype(F32), 0.0)
        mass = jnp.sum(mass, axis=0, keepdims=True)
        mass = jnp.broadcast_to(jnp.concatenate([mass, mass], axis=1), (B, 128))
        wanted = coarse_order(row[:B]) + depth * B
        coarse[y, :, pl.ds(9 * 128, 128)] = jnp.where(wanted == col[:B], mass, 0.0).astype(BF16)
        return carry

    lax.fori_loop(0, size_x, sort_coarse, 0)

    def sent_column(x, carry):
        for sweep in range(1, SWEEPS + 1):
            lateral_do("wait_send", sweep, x)
        return carry

    lateral_do("wait_send", 0, 0)
    lax.fori_loop(0, size_x, sent_column, 0)
    for sweep in range(SWEEPS + 1):
        for side in range(2):
            track_do("wait_send", sweep, side)
    partner.wait()

    def from_fine(y, h):
        r = lax.rem(me - 2 * y - h + group, group)

        @pl.when(r != 0)
        def _():
            pltpu.make_async_remote_copy(
                src_ref=csend.at[y],
                dst_ref=cres.at[h, y],
                send_sem=to_send.at[r],
                recv_sem=to_recv.at[r],
                device_id=(track, y, h),
                device_id_type=MESH,
            ).wait_recv()

    def first_pair(h, pair):
        for k in range(2):
            from_fine(2 * pair + k, h)
        for z in range(2):
            rows = pl.ds(z * B, B)
            stack = [cres[h, 2 * pair + k, rows, :] for k in range(2)]
            block = call[z, pair]
            zero = jnp.zeros_like(block)
            left = jnp.concatenate(
                [jnp.where(low, block, zero), jnp.where(low, zero, block)], axis=0
            )
            value = DAMPING * dot(left, jnp.concatenate(stack, axis=0))
            plain = exact_dot(order, value.astype(BF16))
            for k in range(2):
                first[z, h, 2 * pair + k] = value[k * B : (k + 1) * B]
                cpad[1, h, 2 * pair + k + 1, rows, :] = plain[k * B : (k + 1) * B]

    def side_copy(index, h):
        rows = pl.ds(1, size_l)
        return pltpu.make_async_remote_copy(
            src_ref=cpad.at[1, h, rows],
            dst_ref=cpad.at[2 - 2 * index, h, rows],
            send_sem=side_send.at[index, h],
            recv_sem=side_recv.at[index, h],
            device_id=sides[index][0],
            device_id_type=MESH,
        )

    halves = (depth, 1 - depth)
    for h in halves:
        def first_step(pair, carry, h=h):
            first_pair(h, pair)
            return carry

        lax.fori_loop(0, size_l // 2, first_step, 0)
        for index in range(2):
            @pl.when(sides[index][1])
            def _(index=index, h=h):
                side_copy(index, h).start()

    own_rows = pl.ds(pl.multiple_of(depth * B, B), B)

    def to_fine(y, h):
        r = lax.rem(2 * y + h - me + group, group)
        return r, pltpu.make_async_remote_copy(
            src_ref=csend_back.at[h, y],
            dst_ref=corr.at[depth, lateral],
            send_sem=back_send.at[r],
            recv_sem=back_recv.at[r],
            device_id=(track, y, h),
            device_id_type=MESH,
        )

    for h in halves:
        for index in range(2):
            @pl.when(sides[1 - index][1])
            def _(index=index, h=h):
                side_copy(index, h).wait_recv()

        def coarse_row(y, carry, h=h):
            pieces = [cpad[dx, h, pl.ds(y, 3)].reshape(3 * 128, LD) for dx in range(3)]
            pieces.append(cpad[1, h, y + 1])
            total = dot(coarse[y], jnp.concatenate(pieces, axis=0))
            remain = (cres[h, y, own_rows, :].astype(F32) - total).astype(BF16)
            block = call[depth, y // 2]
            left = jnp.where(low == (lax.rem(y, 2) == 0), block, jnp.zeros_like(block))
            delta = DAMPING * dot(left, jnp.concatenate([remain, remain], axis=0))
            csend_back[h, y] = (first[depth, h, y] + delta).astype(BF16)
            r, copy = to_fine(y, h)

            @pl.when(r != 0)
            def _():
                copy.start()

            return carry

        lax.fori_loop(0, size_l, coarse_row, 0)
    corr[depth, lateral] = csend_back[depth, lateral]

    for index in range(2):
        for h in range(2):
            @pl.when(sides[index][1])
            def _(index=index, h=h):
                side_copy(index, h).wait_send()

    def sent_coarse(y, carry):
        for h in range(2):
            r, copy = to_coarse(y, h)

            @pl.when(r != 0)
            def _(copy=copy):
                copy.wait_send()
        return carry

    lax.fori_loop(0, size_l, sent_coarse, 0)

    def from_coarse(x, carry):
        for z in range(2):
            r = lax.rem(me - 2 * x - z + group, group)

            @pl.when(r != 0)
            def _(z=z, r=r):
                pltpu.make_async_remote_copy(
                    src_ref=csend_back.at[z, x],
                    dst_ref=corr.at[z, x],
                    send_sem=back_send.at[r],
                    recv_sem=back_recv.at[r],
                    device_id=(track, x, z),
                    device_id_type=MESH,
                ).wait_recv()
        return carry

    lax.fori_loop(0, size_x, from_coarse, 0)

    def final_column(x, carry):
        for y in range(2):
            parts = [
                corr[z, table[5 * size_x + 4 + 2 * y + z, x]] for z in range(2)
            ]
            iterate[x, y] += dot(transfer[2 * x + y], jnp.concatenate(parts, axis=0))
            for z in range(2):
                for parity in range(2):
                    rows = every_second(parity * B + z)
                    out[x, y, z, every_second(parity), :] = iterate[x, y, rows, :]
        return carry

    lax.fori_loop(0, size_x, final_column, 0)

    def sent_fine(y, carry):
        for h in range(2):
            r, copy = to_fine(y, h)

            @pl.when(r != 0)
            def _(copy=copy):
                copy.wait_send()
        return carry

    lax.fori_loop(0, size_l, sent_fine, 0)


def run_cycle(
    tracks, rhs, start, fine_blocks, fine_cols, fine_mass, fine_smoother, transfer, aggregate,
    coarse_blocks, coarse_cols, coarse_mass, coarse_smoother,
):
    size_x = rhs.shape[0]
    count = 2 * size_x
    group = 2 * size_x
    tiles = B * B // 128
    fine_blocks = fine_blocks.reshape(size_x, 2, 2, CODES, tiles, 128)
    fine_blocks = jnp.transpose(fine_blocks, (0, 1, 3, 4, 2, 5)).reshape(count, CODES, B, 128)
    pair = []
    for array in (fine_smoother, transfer):
        array = jnp.transpose(array.reshape(size_x, 2, 2, tiles, 128), (0, 1, 3, 2, 4))
        pair.append(array.reshape(count, B, 128))
    coarse_blocks = coarse_blocks.reshape(size_x, CODES, tiles, 128)
    coarse_blocks = jnp.transpose(coarse_blocks, (1, 2, 0, 3)).reshape(CODES, tiles * size_x, 128)
    coarse_smoother = jnp.transpose(coarse_smoother.reshape(size_x, tiles, 128), (1, 0, 2))
    coarse_smoother = coarse_smoother.reshape(tiles * size_x, 128)
    operands = (
        rhs, start, fine_blocks, fine_cols.reshape(2 * count, CODES), fine_mass, *pair,
        jnp.transpose(aggregate, (1, 2, 0)).reshape(4, size_x), coarse_blocks,
        coarse_cols.reshape(size_x, CODES), coarse_mass.reshape(size_x, B), coarse_smoother,
    )
    vmem, dma = pltpu.VMEM, pltpu.SemaphoreType.DMA
    table_rows = 5 * size_x + 8
    return pl.pallas_call(
        functools.partial(cycle_kernel, tracks),
        in_specs=[pl.BlockSpec(memory_space=pl.ANY)] * len(operands),
        out_specs=pl.BlockSpec(memory_space=pltpu.VMEM),
        out_shape=jax.ShapeDtypeStruct(rhs.shape, F32),
        scratch_shapes=[vmem(array.shape, array.dtype) for array in operands] + [
            vmem((table_rows, 128), jnp.int32),
            pltpu.SMEM((table_rows, 128), jnp.int32),
            vmem((count, 128, WIDE), BF16),
            vmem((count, 128, 128), BF16),
            vmem((count, 128, 128), BF16),
            vmem((size_x, B, WIDE), BF16),
            vmem((CODES + 1, tiles * size_x, 128), F32),
            vmem((SWEEPS + 1, size_x + 2, 4, 128, LD), BF16),
            vmem((size_x, 2, 128, LD), F32),
            vmem((size_x, 2, 128, LD), F32),
            vmem((2, size_x, 128, LD), F32),
            vmem((size_x, 128, LD), BF16),
            vmem((2, size_x, 128, LD), BF16),
            vmem((3, 2, size_x + 2, 128, LD), BF16),
            vmem((2, size_x // 2, B, 128), BF16),
            vmem((2, 2, size_x, B, LD), F32),
            vmem((2, size_x, B, LD), BF16),
            vmem((2, size_x, B, LD), BF16),
            dma((11,)), dma((count,)), dma,
            dma((2,)), dma((2,)), dma((SWEEPS, 2, size_x)), dma((SWEEPS, 2, size_x)),
            dma((SWEEPS + 1, 2, 3)), dma((SWEEPS + 1, 2, 3)),
            dma((group,)), dma((group,)), dma((group,)), dma((group,)),
            dma((2, 2)), dma((2, 2)), dma, dma,
        ],
        compiler_params=pltpu.CompilerParams(
            collective_id=0, has_side_effects=True, vmem_limit_bytes=56 << 20
        ),
        name="cycle",
    )(*operands)


def solution(mesh):
    tracks = mesh.shape["track"]

    def per_device(*arrays):
        return run_cycle(tracks, *arrays)

    in_specs = (
        P("track", "lateral", None, None, "depth"),
        P("track", "lateral", None, None, "depth"),
        P("track", "lateral", None, None, None),
        P("track", "lateral", None, None),
        P("track", "lateral", None, None),
        P("track", "lateral", None, None),
        P("track", "lateral", None, None),
        P("track", "lateral", None),
        P(("track", "lateral"), None, "depth", None, None),
        P(("track", "lateral"), None, "depth", None),
        P(("track", "lateral"), None, "depth", None),
        P(("track", "lateral"), None, "depth", None),
    )
    out_specs = P("track", "lateral", None, None, "depth")
    return jax.shard_map(
        per_device, mesh=mesh, in_specs=in_specs, out_specs=out_specs, check_vma=False
    )
```

```python
import functools

import jax
import jax.numpy as jnp
from jax import lax
from jax.experimental import pallas as pl
from jax.experimental.pallas import tpu as pltpu
from jax.sharding import PartitionSpec as P

SWEEPS = 2
DAMPING = 0.8
B = 64
H = B // 2
CODES = 27
LD = 128
WIDE = 10 * 128
F32 = jnp.float32
BF16 = jnp.bfloat16
MESH = pl.DeviceIdType.MESH


def lanes_low(rows):
    return lax.broadcasted_iota(jnp.int32, (rows, 128), 1) < B


def half_swap(block):
    return jnp.concatenate([block[:, B:], block[:, :B]], axis=1)


def even_odd(low, first, second):
    return jnp.where(low, first, half_swap(second)), jnp.where(low, half_swap(first), second)


def fine_order(index):
    return index % 2 * B + index % B // 2 * 2 + index // B


def coarse_order(index):
    return index // B * B + index % H * 2 + index % B // H


def order_matrix(order):
    row = lax.broadcasted_iota(jnp.int32, (128, 128), 0)
    col = lax.broadcasted_iota(jnp.int32, (128, 128), 1)
    return (row == order(col)).astype(F32).astype(BF16)


def exact_dot(left, right):
    return dot(left, right).astype(BF16)


def dot(left, right):
    return jnp.dot(left, right, preferred_element_type=F32)


def every_second(parity):
    return pl.ds(parity, H, stride=2)


def inverse_rows(lists, count):
    rows = lists.shape[0]
    lane = lax.broadcasted_iota(jnp.int32, (rows, 128), 1)
    found = jnp.zeros((rows, 128), jnp.int32)
    for k in range(count):
        found = jnp.where(lists[:, k : k + 1] == lane, k, found)
    return found


def cycle_kernel(
    tracks,
    rhs_hbm, start_hbm, fblk_hbm, fcols_hbm, fmass_hbm, fsm_hbm, tran_hbm, agg_hbm,
    cblk_hbm, ccols_hbm, cmass_hbm, csm_hbm,
    out,
    rhs, start, fblk, fcols, fmass, fsm, tran, agg, cblk, ccols, cmass, csm,
    rows_table, table, fine, smooth, transfer, coarse, spread,
    padded, forces, iterate, projected, csend, cres, cpad, call, first, csend_back, corr,
    load_sem, block_sem, table_sem,
    bulk_send, bulk_recv, lat_send, lat_recv, track_send, track_recv,
    to_send, to_recv, back_send, back_recv, side_send, side_recv, ss_send, ss_recv,
):
    size_x = rhs.shape[0]
    size_l = size_x
    count = 2 * size_x
    group = 2 * size_l
    last = size_x - 1
    track = lax.axis_index("track")
    lateral = lax.axis_index("lateral")
    depth = lax.axis_index("depth")
    me = lateral * 2 + depth

    small = [
        (start_hbm, start), (fcols_hbm, fcols), (ccols_hbm, ccols), (agg_hbm, agg),
        (fmass_hbm, fmass), (fsm_hbm, fsm), (tran_hbm, tran), (rhs_hbm, rhs),
        (csm_hbm, csm), (cmass_hbm, cmass), (cblk_hbm, cblk),
    ]
    loads = [
        pltpu.make_async_copy(source, target, load_sem.at[k])
        for k, (source, target) in enumerate(small)
    ]

    def block_load(i):
        return pltpu.make_async_copy(fblk_hbm.at[i], fblk.at[i], block_sem.at[i])

    for load in loads[:8]:
        load.start()

    def start_block(i, carry):
        block_load(i).start()
        return carry

    lax.fori_loop(0, count, start_block, 0)
    for load in loads[8:]:
        load.start()

    def exists(dt, dl):
        ok = None
        for step, at, ends in ((dt, track, tracks), (dl, lateral, size_l)):
            if step:
                here = (at > 0) if step < 0 else (at < ends - 1)
                ok = here if ok is None else jnp.logical_and(ok, here)
        return ok

    at_first = (lateral == 0).astype(jnp.int32)
    at_last = (lateral == last).astype(jnp.int32)
    before = (track - at_first, lax.rem(lateral + last, size_l), lax.rem(depth + at_first, 2))
    after = (track + at_last, lax.rem(lateral + 1, size_l), lax.rem(depth + at_last, 2))
    sides = (
        (before, jnp.logical_or(track > 0, lateral > 0)),
        (after, jnp.logical_or(track < tracks - 1, lateral < last)),
    )

    for sweep in range(SWEEPS + 1):
        for place in (0, size_x + 1):
            padded[sweep, place] = jnp.zeros_like(padded[sweep, place])
        for place in (0, 3):
            padded[sweep, :, place] = jnp.zeros_like(padded[sweep, :, place])
    for place in (0, 2):
        cpad[place] = jnp.zeros_like(cpad[place])
    for place in (0, size_l + 1):
        cpad[1, :, place] = jnp.zeros_like(cpad[1, :, place])

    barrier = pltpu.get_barrier_semaphore()
    for r in range(1, group):
        other = lax.rem(me + r, group)
        pl.semaphore_signal(
            barrier, inc=1, device_id=(track, other // 2, lax.rem(other, 2)), device_id_type=MESH
        )
    expected = group - 1
    for dt in (-1, 1):
        for dl in (-1, 0, 1):
            ok = exists(dt, dl)

            @pl.when(ok)
            def _(dt=dt, dl=dl):
                pl.semaphore_signal(
                    barrier, inc=1, device_id=(track + dt, lateral + dl, depth), device_id_type=MESH
                )

            expected = expected + ok.astype(jnp.int32)
    for (device, ok), at_end in zip(sides, (lateral == 0, lateral == last)):
        crossing = jnp.logical_and(ok, at_end)

        @pl.when(crossing)
        def _(device=device):
            pl.semaphore_signal(barrier, inc=1, device_id=device, device_id_type=MESH)

        expected = expected + crossing.astype(jnp.int32)

    def round_start(x, carry):
        for y in range(2):
            for z in range(2):
                padded[0, x + 1, y + 1, pl.ds(z * B, B), :] = start[x, y, z].astype(BF16)
        return carry

    loads[0].wait()
    lax.fori_loop(0, size_x, round_start, 0)
    pl.semaphore_wait(barrier, expected)

    def lateral_copy(sweep, x, side):
        if sweep == 0:
            columns, sems = pl.ds(1, size_x), (bulk_send.at[side], bulk_recv.at[side])
        else:
            sems = (lat_send.at[sweep - 1, side, x], lat_recv.at[sweep - 1, side, x])
            columns = x + 1
        return pltpu.make_async_remote_copy(
            src_ref=padded.at[sweep, columns, 1 + side],
            dst_ref=padded.at[sweep, columns, 3 - 3 * side],
            send_sem=sems[0],
            recv_sem=sems[1],
            device_id=(track, lateral + 2 * side - 1, depth),
            device_id_type=MESH,
        )

    def track_copy(sweep, side, dl):
        src_y, dst_y = {0: (pl.ds(1, 2),) * 2, -1: (1, 3), 1: (2, 0)}[dl]
        return pltpu.make_async_remote_copy(
            src_ref=padded.at[sweep, size_x if side else 1, src_y],
            dst_ref=padded.at[sweep, 0 if side else size_x + 1, dst_y],
            send_sem=track_send.at[sweep, side, dl + 1],
            recv_sem=track_recv.at[sweep, side, dl + 1],
            device_id=(track + 2 * side - 1, lateral + dl, depth),
            device_id_type=MESH,
        )

    def lateral_do(action, sweep, x):
        for side in range(2):
            step = 2 * side - 1

            @pl.when(exists(0, -step if action == "wait_recv" else step))
            def _(side=side):
                getattr(lateral_copy(sweep, x, side), action)()

    def track_do(action, sweep, side):
        step = 2 * side - 1
        for dl in (0, -1, 1):
            here = (-step, -dl) if action == "wait_recv" else (step, dl)

            @pl.when(exists(*here))
            def _(dl=dl):
                getattr(track_copy(sweep, side, dl), action)()

    lateral_do("start", 0, 0)
    for side in range(2):
        track_do("start", 0, side)

    for load in loads[1:4]:
        load.wait()
    rows_table[pl.ds(0, 4 * size_x), :] = inverse_rows(fcols[...], CODES)
    rows_table[pl.ds(4 * size_x, size_x), :] = inverse_rows(ccols[...], CODES)
    groups = lax.rem(agg[...], size_x)
    rows_table[pl.ds(5 * size_x, 4), :] = inverse_rows(groups, size_x)
    rows_table[pl.ds(5 * size_x + 4, 4), pl.ds(0, size_x)] = groups
    fill = pltpu.make_async_copy(rows_table, table, table_sem)
    fill.start()
    for load in loads[4:9]:
        load.wait()

    def reorder(x, carry):
        for y in range(2):
            for z in range(2):
                for parity in range(2):
                    rows = every_second(parity * B + z)
                    for source, target in ((rhs, forces), (start, iterate)):
                        target[x, y, rows, :] = source[x, y, z, every_second(parity), :]
        return carry

    lax.fori_loop(0, size_x, reorder, 0)
    swap = order_matrix(fine_order)
    order = order_matrix(coarse_order)
    low = lanes_low(B)
    upper = lax.broadcasted_iota(jnp.int32, (B, 128), 0) % 2 == 0
    row = lax.broadcasted_iota(jnp.int32, (128, 128), 0)
    col = lax.broadcasted_iota(jnp.int32, (128, 128), 1)

    spread[CODES] = csm[...].astype(F32)
    for pair in range(size_x // 2):
        parts = [spread[CODES, pl.ds(2 * pair + k, H, stride=size_x), :] for k in range(2)]
        even, odd = even_odd(low[:H], *parts)
        both = jnp.concatenate([even, odd], axis=0).astype(BF16)
        call[depth, pair] = exact_dot(both, order)
    partner = pltpu.make_async_remote_copy(
        src_ref=call.at[depth],
        dst_ref=call.at[depth],
        send_sem=ss_send,
        recv_sem=ss_recv,
        device_id=(track, lateral, 1 - depth),
        device_id_type=MESH,
    )
    partner.start()
    fill.wait()

    def wait_block(i, carry):
        block_load(i).wait()
        return carry

    lax.fori_loop(0, count, wait_block, 0)

    def sort_fine(i, carry):
        def block(layer, code):
            return fblk[i, table[2 * i + layer, code]]

        for near in range(9):
            code = near * 3 + 1
            one = jnp.where(upper, block(0, code), block(1, code - 1))
            two = jnp.where(upper, block(0, code + 1), block(1, code))
            even, odd = even_odd(low, one, two)
            at = pl.ds(near * 128, 128)
            fine[i, pl.ds(0, B), at] = even
            fine[i, pl.ds(B, B), at] = odd
        mass = fmass[i // 2, lax.rem(i, 2)].astype(F32)
        mass = jnp.concatenate([mass[0:1], mass[1:2]], axis=1)
        diag = jnp.where(fine_order(row) == col, jnp.broadcast_to(mass, (128, 128)), 0.0)
        fine[i, :, pl.ds(9 * 128, 128)] = diag.astype(BF16)
        for source, target, reordering in ((fsm, smooth, swap), (tran, transfer, order)):
            whole = source[i]
            zero = jnp.zeros_like(whole)
            even, odd = even_odd(low, jnp.where(upper, whole, zero), jnp.where(upper, zero, whole))
            target[i] = exact_dot(jnp.concatenate([even, odd], axis=0), reordering)
        return carry

    lax.fori_loop(0, count, sort_fine, 0)
    lateral_do("wait_recv", 0, 0)
    for side in range(2):
        track_do("wait_recv", 0, side)

    def apply_fine(sweep, x, y):
        pieces = [
            padded[sweep, x + dx, pl.ds(y, 3)].reshape(3 * 128, LD) for dx in range(3)
        ]
        pieces.append(padded[sweep, x + 1, y + 1])
        return dot(fine[2 * x + y], jnp.concatenate(pieces, axis=0))

    def smooth_column(sweep, x):
        totals = [apply_fine(sweep, x, y) for y in range(2)]
        res = [(forces[x, y] - totals[y]).astype(BF16) for y in range(2)]
        steps = [DAMPING * dot(smooth[2 * x + y], res[y]) for y in range(2)]
        for y in range(2):
            new = iterate[x, y] + steps[y]
            iterate[x, y] = new
            padded[sweep + 1, x + 1, y + 1] = exact_dot(swap, new.astype(BF16))
        lateral_do("start", sweep + 1, x)

        @pl.when(x == 0)
        def _():
            track_do("start", sweep + 1, 0)

        @pl.when(x == last)
        def _():
            track_do("start", sweep + 1, 1)

    def outer_first(i, carry):
        x = i - 1 + (i == 0).astype(jnp.int32) + (i == 1).astype(jnp.int32) * last
        smooth_column(0, x)
        return carry

    lax.fori_loop(0, size_x, outer_first, 0)

    def in_order(x, carry):
        @pl.when(x == 0)
        def _():
            lateral_do("wait_recv", 1, 0)
            track_do("wait_recv", 1, 1)

        @pl.when(x < last)
        def _():
            lateral_do("wait_recv", 1, x + 1)

        @pl.when(x == last)
        def _():
            track_do("wait_recv", 1, 0)

        smooth_column(1, x)
        return carry

    lax.fori_loop(0, size_x, in_order, 0)

    def project_column(i, carry):
        x = lax.rem(i + 1, size_x)

        @pl.when(i == 0)
        def _():
            lateral_do("wait_recv", 2, 0)
            lateral_do("wait_recv", 2, 1)

        @pl.when(jnp.logical_and(x > 0, x < last))
        def _():
            lateral_do("wait_recv", 2, x + 1)

        @pl.when(x == last)
        def _():
            track_do("wait_recv", 2, 0)

        @pl.when(x == 0)
        def _():
            track_do("wait_recv", 2, 1)

        for y in range(2):
            res = (forces[x, y] - apply_fine(SWEEPS, x, y)).astype(BF16)
            projected[y, x] = lax.dot_general(
                transfer[2 * x + y], res, (((0,), (0,)), ((), ())), preferred_element_type=F32
            )
        return carry

    lax.fori_loop(0, size_x, project_column, 0)

    def to_coarse(other_l, other_d):
        r = lax.rem(other_l * 2 + other_d - me + group, group)
        return r, pltpu.make_async_remote_copy(
            src_ref=csend.at[other_l],
            dst_ref=cres.at[depth, lateral],
            send_sem=to_send.at[r],
            recv_sem=to_recv.at[r],
            device_id=(track, other_l, other_d),
            device_id_type=MESH,
        )

    def group_column(a, carry):
        for z in range(2):
            rows = pl.ds(z * B, B)
            total = (
                projected[0, table[5 * size_x + z, a], rows, :]
                + projected[1, table[5 * size_x + 2 + z, a], rows, :]
            )
            csend[a, rows, :] = total.astype(BF16)
        for other_d in range(2):
            r, copy = to_coarse(a, other_d)

            @pl.when(r != 0)
            def _(copy=copy):
                copy.start()
        return carry

    lax.fori_loop(0, size_x, group_column, 0)
    cres[depth, lateral] = csend[lateral]

    for load in loads[9:]:
        load.wait()

    def widen(slot, carry):
        spread[slot] = cblk[slot].astype(F32)
        return carry

    lax.fori_loop(0, CODES, widen, 0)

    def sort_coarse(y, carry):
        for near in range(9):
            parts = []
            for z in range(2):
                slot = table[4 * size_x + y, near * 3 + 1 + z - depth]
                parts.append(spread[slot, pl.ds(y, H, stride=size_x), :])
            even, odd = even_odd(low[:H], *parts)
            at = pl.ds(near * 128, 128)
            coarse[y, pl.ds(0, H), at] = even.astype(BF16)
            coarse[y, pl.ds(H, H), at] = odd.astype(BF16)
        chosen = lax.broadcasted_iota(jnp.int32, (size_x, B), 0) == y
        mass = jnp.where(chosen, cmass[...].astype(F32), 0.0)
        mass = jnp.sum(mass, axis=0, keepdims=True)
        mass = jnp.broadcast_to(jnp.concatenate([mass, mass], axis=1), (B, 128))
        wanted = coarse_order(row[:B]) + depth * B
        coarse[y, :, pl.ds(9 * 128, 128)] = jnp.where(wanted == col[:B], mass, 0.0).astype(BF16)
        return carry

    lax.fori_loop(0, size_x, sort_coarse, 0)

    def sent_column(x, carry):
        for sweep in range(1, SWEEPS + 1):
            lateral_do("wait_send", sweep, x)
        return carry

    lateral_do("wait_send", 0, 0)
    lax.fori_loop(0, size_x, sent_column, 0)
    for sweep in range(SWEEPS + 1):
        for side in range(2):
            track_do("wait_send", sweep, side)
    partner.wait()

    def from_fine(y, h):
        r = lax.rem(me - 2 * y - h + group, group)

        @pl.when(r != 0)
        def _():
            pltpu.make_async_remote_copy(
                src_ref=csend.at[y],
                dst_ref=cres.at[h, y],
                send_sem=to_send.at[r],
                recv_sem=to_recv.at[r],
                device_id=(track, y, h),
                device_id_type=MESH,
            ).wait_recv()

    def first_pair(h, pair):
        for k in range(2):
            from_fine(2 * pair + k, h)
        for z in range(2):
            rows = pl.ds(z * B, B)
            stack = [cres[h, 2 * pair + k, rows, :] for k in range(2)]
            block = call[z, pair]
            zero = jnp.zeros_like(block)
            left = jnp.concatenate(
                [jnp.where(low, block, zero), jnp.where(low, zero, block)], axis=0
            )
            value = DAMPING * dot(left, jnp.concatenate(stack, axis=0))
            plain = exact_dot(order, value.astype(BF16))
            for k in range(2):
                first[z, h, 2 * pair + k] = value[k * B : (k + 1) * B]
                cpad[1, h, 2 * pair + k + 1, rows, :] = plain[k * B : (k + 1) * B]

    def side_copy(index, h):
        rows = pl.ds(1, size_l)
        return pltpu.make_async_remote_copy(
            src_ref=cpad.at[1, h, rows],
            dst_ref=cpad.at[2 - 2 * index, h, rows],
            send_sem=side_send.at[index, h],
            recv_sem=side_recv.at[index, h],
            device_id=sides[index][0],
            device_id_type=MESH,
        )

    halves = (depth, 1 - depth)
    for h in halves:
        def first_step(pair, carry, h=h):
            first_pair(h, pair)
            return carry

        lax.fori_loop(0, size_l // 2, first_step, 0)
        for index in range(2):
            @pl.when(sides[index][1])
            def _(index=index, h=h):
                side_copy(index, h).start()

    own_rows = pl.ds(pl.multiple_of(depth * B, B), B)

    def to_fine(y, h):
        r = lax.rem(2 * y + h - me + group, group)
        return r, pltpu.make_async_remote_copy(
            src_ref=csend_back.at[h, y],
            dst_ref=corr.at[depth, lateral],
            send_sem=back_send.at[r],
            recv_sem=back_recv.at[r],
            device_id=(track, y, h),
            device_id_type=MESH,
        )

    for h in halves:
        for index in range(2):
            @pl.when(sides[1 - index][1])
            def _(index=index, h=h):
                side_copy(index, h).wait_recv()

        def coarse_row(y, carry, h=h):
            pieces = [cpad[dx, h, pl.ds(y, 3)].reshape(3 * 128, LD) for dx in range(3)]
            pieces.append(cpad[1, h, y + 1])
            total = dot(coarse[y], jnp.concatenate(pieces, axis=0))
            remain = (cres[h, y, own_rows, :].astype(F32) - total).astype(BF16)
            block = call[depth, y // 2]
            left = jnp.where(low == (lax.rem(y, 2) == 0), block, jnp.zeros_like(block))
            delta = DAMPING * dot(left, jnp.concatenate([remain, remain], axis=0))
            csend_back[h, y] = (first[depth, h, y] + delta).astype(BF16)
            r, copy = to_fine(y, h)

            @pl.when(r != 0)
            def _():
                copy.start()

            return carry

        lax.fori_loop(0, size_l, coarse_row, 0)
    corr[depth, lateral] = csend_back[depth, lateral]

    for index in range(2):
        for h in range(2):
            @pl.when(sides[index][1])
            def _(index=index, h=h):
                side_copy(index, h).wait_send()

    def sent_coarse(y, carry):
        for h in range(2):
            r, copy = to_coarse(y, h)

            @pl.when(r != 0)
            def _(copy=copy):
                copy.wait_send()
        return carry

    lax.fori_loop(0, size_l, sent_coarse, 0)

    def from_coarse(x, carry):
        for z in range(2):
            r = lax.rem(me - 2 * x - z + group, group)

            @pl.when(r != 0)
            def _(z=z, r=r):
                pltpu.make_async_remote_copy(
                    src_ref=csend_back.at[z, x],
                    dst_ref=corr.at[z, x],
                    send_sem=back_send.at[r],
                    recv_sem=back_recv.at[r],
                    device_id=(track, x, z),
                    device_id_type=MESH,
                ).wait_recv()
        return carry

    lax.fori_loop(0, size_x, from_coarse, 0)

    def final_column(x, carry):
        for y in range(2):
            parts = [
                corr[z, table[5 * size_x + 4 + 2 * y + z, x]] for z in range(2)
            ]
            iterate[x, y] += dot(transfer[2 * x + y], jnp.concatenate(parts, axis=0))
            for z in range(2):
                for parity in range(2):
                    rows = every_second(parity * B + z)
                    out[x, y, z, every_second(parity), :] = iterate[x, y, rows, :]
        return carry

    lax.fori_loop(0, size_x, final_column, 0)

    def sent_fine(y, carry):
        for h in range(2):
            r, copy = to_fine(y, h)

            @pl.when(r != 0)
            def _(copy=copy):
                copy.wait_send()
        return carry

    lax.fori_loop(0, size_l, sent_fine, 0)


def run_cycle(
    tracks, rhs, start, fine_blocks, fine_cols, fine_mass, fine_smoother, transfer, aggregate,
    coarse_blocks, coarse_cols, coarse_mass, coarse_smoother,
):
    size_x = rhs.shape[0]
    count = 2 * size_x
    group = 2 * size_x
    tiles = B * B // 128
    fine_blocks = fine_blocks.reshape(size_x, 2, 2, CODES, tiles, 128)
    fine_blocks = jnp.transpose(fine_blocks, (0, 1, 3, 4, 2, 5)).reshape(count, CODES, B, 128)
    pair = []
    for array in (fine_smoother, transfer):
        array = jnp.transpose(array.reshape(size_x, 2, 2, tiles, 128), (0, 1, 3, 2, 4))
        pair.append(array.reshape(count, B, 128))
    coarse_blocks = coarse_blocks.reshape(size_x, CODES, tiles, 128)
    coarse_blocks = jnp.transpose(coarse_blocks, (1, 2, 0, 3)).reshape(CODES, tiles * size_x, 128)
    coarse_smoother = jnp.transpose(coarse_smoother.reshape(size_x, tiles, 128), (1, 0, 2))
    coarse_smoother = coarse_smoother.reshape(tiles * size_x, 128)
    operands = (
        rhs, start, fine_blocks, fine_cols.reshape(2 * count, CODES), fine_mass, *pair,
        jnp.transpose(aggregate, (1, 2, 0)).reshape(4, size_x), coarse_blocks,
        coarse_cols.reshape(size_x, CODES), coarse_mass.reshape(size_x, B), coarse_smoother,
    )
    vmem, dma = pltpu.VMEM, pltpu.SemaphoreType.DMA
    table_rows = 5 * size_x + 8
    return pl.pallas_call(
        functools.partial(cycle_kernel, tracks),
        in_specs=[pl.BlockSpec(memory_space=pl.ANY)] * len(operands),
        out_specs=pl.BlockSpec(memory_space=pltpu.VMEM),
        out_shape=jax.ShapeDtypeStruct(rhs.shape, F32),
        scratch_shapes=[vmem(array.shape, array.dtype) for array in operands] + [
            vmem((table_rows, 128), jnp.int32),
            pltpu.SMEM((table_rows, 128), jnp.int32),
            vmem((count, 128, WIDE), BF16),
            vmem((count, 128, 128), BF16),
            vmem((count, 128, 128), BF16),
            vmem((size_x, B, WIDE), BF16),
            vmem((CODES + 1, tiles * size_x, 128), F32),
            vmem((SWEEPS + 1, size_x + 2, 4, 128, LD), BF16),
            vmem((size_x, 2, 128, LD), F32),
            vmem((size_x, 2, 128, LD), F32),
            vmem((2, size_x, 128, LD), F32),
            vmem((size_x, 128, LD), BF16),
            vmem((2, size_x, 128, LD), BF16),
            vmem((3, 2, size_x + 2, 128, LD), BF16),
            vmem((2, size_x // 2, B, 128), BF16),
            vmem((2, 2, size_x, B, LD), F32),
            vmem((2, size_x, B, LD), BF16),
            vmem((2, size_x, B, LD), BF16),
            dma((11,)), dma((count,)), dma,
            dma((2,)), dma((2,)), dma((SWEEPS, 2, size_x)), dma((SWEEPS, 2, size_x)),
            dma((SWEEPS + 1, 2, 3)), dma((SWEEPS + 1, 2, 3)),
            dma((group,)), dma((group,)), dma((group,)), dma((group,)),
            dma((2, 2)), dma((2, 2)), dma, dma,
        ],
        compiler_params=pltpu.CompilerParams(
            collective_id=0, has_side_effects=True, vmem_limit_bytes=56 << 20
        ),
        name="cycle",
    )(*operands)


def solution(mesh):
    tracks = mesh.shape["track"]

    def per_device(*arrays):
        return run_cycle(tracks, *arrays)

    in_specs = (
        P("track", "lateral", None, None, "depth"),
        P("track", "lateral", None, None, "depth"),
        P("track", "lateral", None, None, None),
        P("track", "lateral", None, None),
        P("track", "lateral", None, None),
        P("track", "lateral", None, None),
        P("track", "lateral", None, None),
        P("track", "lateral", None),
        P(("track", "lateral"), None, "depth", None, None),
        P(("track", "lateral"), None, "depth", None),
        P(("track", "lateral"), None, "depth", None),
        P(("track", "lateral"), None, "depth", None),
    )
    out_specs = P("track", "lateral", None, None, "depth")
    return jax.shard_map(
        per_device, mesh=mesh, in_specs=in_specs, out_specs=out_specs, check_vma=False
    )
```

```python
import functools

import jax
import jax.numpy as jnp
from jax import lax
from jax.experimental import pallas as pl
from jax.experimental.pallas import tpu as pltpu
from jax.sharding import PartitionSpec as P

SWEEPS = 2
DAMPING = 0.8
B = 64
H = B // 2
CODES = 27
LD = 128
WIDE = 10 * 128
F32 = jnp.float32
BF16 = jnp.bfloat16
MESH = pl.DeviceIdType.MESH


def lanes_low(rows):
    return lax.broadcasted_iota(jnp.int32, (rows, 128), 1) < B


def half_swap(block):
    return jnp.concatenate([block[:, B:], block[:, :B]], axis=1)


def even_odd(low, first, second):
    return jnp.where(low, first, half_swap(second)), jnp.where(low, half_swap(first), second)


def fine_order(index):
    return index % 2 * B + index % B // 2 * 2 + index // B


def coarse_order(index):
    return index // B * B + index % H * 2 + index % B // H


def order_matrix(order):
    row = lax.broadcasted_iota(jnp.int32, (128, 128), 0)
    col = lax.broadcasted_iota(jnp.int32, (128, 128), 1)
    return (row == order(col)).astype(F32).astype(BF16)


def exact_dot(left, right):
    return dot(left, right).astype(BF16)


def dot(left, right):
    return jnp.dot(left, right, preferred_element_type=F32)


def every_second(parity):
    return pl.ds(parity, H, stride=2)


def inverse_rows(lists, count):
    rows = lists.shape[0]
    lane = lax.broadcasted_iota(jnp.int32, (rows, 128), 1)
    found = jnp.zeros((rows, 128), jnp.int32)
    for k in range(count):
        found = jnp.where(lists[:, k : k + 1] == lane, k, found)
    return found


def cycle_kernel(
    tracks,
    rhs_hbm, start_hbm, fblk_hbm, fcols_hbm, fmass_hbm, fsm_hbm, tran_hbm, agg_hbm,
    cblk_hbm, ccols_hbm, cmass_hbm, csm_hbm,
    out,
    rhs, start, fblk, fcols, fmass, fsm, tran, agg, cblk, ccols, cmass, csm,
    rows_table, table, fine, smooth, transfer, coarse, spread,
    padded, forces, iterate, projected, csend, cres, cpad, call, first, csend_back, corr,
    load_sem, block_sem, table_sem,
    lat_send, lat_recv, track_send, track_recv,
    to_send, to_recv, back_send, back_recv, side_send, side_recv, ss_send, ss_recv,
):
    size_x = rhs.shape[0]
    size_l = size_x
    count = 2 * size_x
    group = 2 * size_l
    last = size_x - 1
    track = lax.axis_index("track")
    lateral = lax.axis_index("lateral")
    depth = lax.axis_index("depth")
    me = lateral * 2 + depth

    def exists(dt, dl):
        ok = None
        for step, at, ends in ((dt, track, tracks), (dl, lateral, size_l)):
            if step:
                here = (at > 0) if step < 0 else (at < ends - 1)
                ok = here if ok is None else jnp.logical_and(ok, here)
        return ok

    at_first = (lateral == 0).astype(jnp.int32)
    at_last = (lateral == last).astype(jnp.int32)
    before = (track - at_first, lax.rem(lateral + last, size_l), lax.rem(depth + at_first, 2))
    after = (track + at_last, lax.rem(lateral + 1, size_l), lax.rem(depth + at_last, 2))
    sides = (
        (before, jnp.logical_or(track > 0, lateral > 0)),
        (after, jnp.logical_or(track < tracks - 1, lateral < last)),
    )

    barrier = pltpu.get_barrier_semaphore()
    for r in range(1, group):
        other = lax.rem(me + r, group)
        pl.semaphore_signal(
            barrier, inc=1, device_id=(track, other // 2, lax.rem(other, 2)), device_id_type=MESH
        )
    expected = group - 1
    for dt in (-1, 1):
        for dl in (-1, 0, 1):
            ok = exists(dt, dl)

            @pl.when(ok)
            def _(dt=dt, dl=dl):
                pl.semaphore_signal(
                    barrier, inc=1, device_id=(track + dt, lateral + dl, depth), device_id_type=MESH
                )

            expected = expected + ok.astype(jnp.int32)
    for (device, ok), at_end in zip(sides, (lateral == 0, lateral == last)):
        crossing = jnp.logical_and(ok, at_end)

        @pl.when(crossing)
        def _(device=device):
            pl.semaphore_signal(barrier, inc=1, device_id=device, device_id_type=MESH)

        expected = expected + crossing.astype(jnp.int32)

    small = [
        (start_hbm, start), (fcols_hbm, fcols), (ccols_hbm, ccols), (agg_hbm, agg),
        (fmass_hbm, fmass), (fsm_hbm, fsm), (tran_hbm, tran), (rhs_hbm, rhs),
        (csm_hbm, csm), (cmass_hbm, cmass), (cblk_hbm, cblk),
    ]
    loads = [
        pltpu.make_async_copy(source, target, load_sem.at[k])
        for k, (source, target) in enumerate(small)
    ]

    def block_load(i):
        return pltpu.make_async_copy(fblk_hbm.at[i], fblk.at[i], block_sem.at[i])

    for load in loads[:8]:
        load.start()

    def start_block(i, carry):
        block_load(i).start()
        return carry

    lax.fori_loop(0, count, start_block, 0)
    for load in loads[8:]:
        load.start()

    def clear(ref, *places):
        for place in places:
            ref[place] = jnp.zeros_like(ref[place])

    every = slice(None)
    for missing, place in (
        (track == 0, (0,)), (track == tracks - 1, (size_x + 1,)),
        (lateral == 0, (every, 0)), (lateral == last, (every, 3)),
    ):
        @pl.when(missing)
        def _(place=place):
            clear(padded, *[(sweep,) + place for sweep in range(SWEEPS + 1)])

    def round_start(x, carry):
        for y in range(2):
            for z in range(2):
                padded[0, x + 1, y + 1, pl.ds(z * B, B), :] = start[x, y, z].astype(BF16)
        return carry

    loads[0].wait()
    lax.fori_loop(0, size_x, round_start, 0)
    pl.semaphore_wait(barrier, expected)

    def lateral_copy(sweep, x, side):
        columns = x + 1
        return pltpu.make_async_remote_copy(
            src_ref=padded.at[sweep, columns, 1 + side],
            dst_ref=padded.at[sweep, columns, 3 - 3 * side],
            send_sem=lat_send.at[sweep, side, x],
            recv_sem=lat_recv.at[sweep, side, x],
            device_id=(track, lateral + 2 * side - 1, depth),
            device_id_type=MESH,
        )

    def track_copy(sweep, side, dl):
        src_y, dst_y = {0: (pl.ds(1, 2),) * 2, -1: (1, 3), 1: (2, 0)}[dl]
        return pltpu.make_async_remote_copy(
            src_ref=padded.at[sweep, size_x if side else 1, src_y],
            dst_ref=padded.at[sweep, 0 if side else size_x + 1, dst_y],
            send_sem=track_send.at[sweep, side, dl + 1],
            recv_sem=track_recv.at[sweep, side, dl + 1],
            device_id=(track + 2 * side - 1, lateral + dl, depth),
            device_id_type=MESH,
        )

    def lateral_do(action, sweep, x):
        for side in range(2):
            step = 2 * side - 1

            @pl.when(exists(0, -step if action == "wait_recv" else step))
            def _(side=side):
                getattr(lateral_copy(sweep, x, side), action)()

    def track_do(action, sweep, side):
        step = 2 * side - 1
        for dl in (0, -1, 1):
            here = (-step, -dl) if action == "wait_recv" else (step, dl)

            @pl.when(exists(*here))
            def _(dl=dl):
                getattr(track_copy(sweep, side, dl), action)()

    pairs = size_x // 2
    outer_first = list(dict.fromkeys([0, pairs - 1] + list(range(pairs))))
    inner_first = list(range(1, pairs)) + [0]
    ahead = {}
    for sweep, sequence in enumerate((outer_first, list(range(pairs)), inner_first)):
        known = set()
        for p in sequence:
            wanted = [x for x in range(2 * p - 1, 2 * p + 3) if 0 <= x <= last]
            ahead[sweep, p] = [x for x in wanted if x not in known]
            known.update(wanted)

    for side in range(2):
        track_do("start", 0, side)
    for p in outer_first:
        for x in ahead[0, p]:
            lateral_do("start", 0, x)

    for load in loads[1:4]:
        load.wait()
    rows_table[pl.ds(0, 4 * size_x), :] = inverse_rows(fcols[...], CODES)
    rows_table[pl.ds(4 * size_x, size_x), :] = inverse_rows(ccols[...], CODES)
    groups = lax.rem(agg[...], size_x)
    rows_table[pl.ds(5 * size_x, 4), :] = inverse_rows(groups, size_x)
    rows_table[pl.ds(5 * size_x + 4, 4), pl.ds(0, size_x)] = groups
    fill = pltpu.make_async_copy(rows_table, table, table_sem)
    fill.start()
    for load in loads[4:9]:
        load.wait()

    def reorder(x, carry):
        for y in range(2):
            for z in range(2):
                for parity in range(2):
                    rows = every_second(parity * B + z)
                    for source, target in ((rhs, forces), (start, iterate)):
                        target[x, y, rows, :] = source[x, y, z, every_second(parity), :]
        return carry

    lax.fori_loop(0, size_x, reorder, 0)
    swap = order_matrix(fine_order)
    order = order_matrix(coarse_order)
    low = lanes_low(B)
    upper = lax.broadcasted_iota(jnp.int32, (B, 128), 0) % 2 == 0
    row = lax.broadcasted_iota(jnp.int32, (128, 128), 0)
    col = lax.broadcasted_iota(jnp.int32, (128, 128), 1)

    spread[CODES] = csm[...].astype(F32)
    for pair in range(size_x // 2):
        parts = [spread[CODES, pl.ds(2 * pair + k, H, stride=size_x), :] for k in range(2)]
        even, odd = even_odd(low[:H], *parts)
        both = jnp.concatenate([even, odd], axis=0).astype(BF16)
        call[depth, pair] = exact_dot(both, order)
    partner = pltpu.make_async_remote_copy(
        src_ref=call.at[depth],
        dst_ref=call.at[depth],
        send_sem=ss_send,
        recv_sem=ss_recv,
        device_id=(track, lateral, 1 - depth),
        device_id_type=MESH,
    )
    fill.wait()

    def wait_block(i, carry):
        block_load(i).wait()
        return carry

    lax.fori_loop(0, count, wait_block, 0)

    def sort_fine(i, carry):
        def block(layer, code):
            return fblk[i, table[2 * i + layer, code]]

        for near in range(9):
            code = near * 3 + 1
            one = jnp.where(upper, block(0, code), block(1, code - 1))
            two = jnp.where(upper, block(0, code + 1), block(1, code))
            even, odd = even_odd(low, one, two)
            at = pl.ds(near * 128, 128)
            fine[i, pl.ds(0, B), at] = even
            fine[i, pl.ds(B, B), at] = odd
        mass = fmass[i // 2, lax.rem(i, 2)].astype(F32)
        mass = jnp.concatenate([mass[0:1], mass[1:2]], axis=1)
        diag = jnp.where(fine_order(row) == col, jnp.broadcast_to(mass, (128, 128)), 0.0)
        fine[i, :, pl.ds(9 * 128, 128)] = diag.astype(BF16)
        for source, target, reordering in ((fsm, smooth, swap), (tran, transfer, order)):
            whole = source[i]
            zero = jnp.zeros_like(whole)
            even, odd = even_odd(low, jnp.where(upper, whole, zero), jnp.where(upper, zero, whole))
            target[i] = exact_dot(jnp.concatenate([even, odd], axis=0), reordering)
        return carry

    lax.fori_loop(0, count, sort_fine, 0)
    def apply_fine(sweep, x, y):
        pieces = [
            padded[sweep, x + dx, pl.ds(y, 3)].reshape(3 * 128, LD) for dx in range(3)
        ]
        pieces.append(padded[sweep, x + 1, y + 1])
        return dot(fine[2 * x + y], jnp.concatenate(pieces, axis=0))

    def await_halo(sweep, p):
        if p == 0:
            track_do("wait_recv", sweep, 1)
        if p == pairs - 1:
            track_do("wait_recv", sweep, 0)
        for x in ahead[sweep, p]:
            lateral_do("wait_recv", sweep, x)

    def cells(p):
        return [(x, y) for x in (2 * p, 2 * p + 1) for y in range(2)]

    for sweep, sequence in enumerate((outer_first, range(pairs))):
        for p in sequence:
            await_halo(sweep, p)
            totals = [apply_fine(sweep, x, y) for x, y in cells(p)]
            res = [(forces[x, y] - t).astype(BF16) for (x, y), t in zip(cells(p), totals)]
            steps = [DAMPING * dot(smooth[2 * x + y], r) for (x, y), r in zip(cells(p), res)]
            news = [iterate[x, y] + step for (x, y), step in zip(cells(p), steps)]
            plain = [exact_dot(swap, new.astype(BF16)) for new in news]
            for (x, y), new, rounded in zip(cells(p), news, plain):
                iterate[x, y] = new
                padded[sweep + 1, x + 1, y + 1] = rounded
            if p == 0:
                track_do("start", sweep + 1, 0)
            if p == pairs - 1:
                track_do("start", sweep + 1, 1)
            for x in (2 * p, 2 * p + 1):
                lateral_do("start", sweep + 1, x)

    partner.start()
    for p in inner_first:
        await_halo(SWEEPS, p)
        totals = [apply_fine(SWEEPS, x, y) for x, y in cells(p)]
        res = [(forces[x, y] - t).astype(BF16) for (x, y), t in zip(cells(p), totals)]
        for (x, y), r in zip(cells(p), res):
            projected[y, x] = lax.dot_general(
                transfer[2 * x + y], r, (((0,), (0,)), ((), ())), preferred_element_type=F32
            )

    def to_coarse(other_l, other_d):
        r = lax.rem(other_l * 2 + other_d - me + group, group)
        return r, pltpu.make_async_remote_copy(
            src_ref=csend.at[other_l],
            dst_ref=cres.at[depth, lateral],
            send_sem=to_send.at[r],
            recv_sem=to_recv.at[r],
            device_id=(track, other_l, other_d),
            device_id_type=MESH,
        )

    def group_column(a, carry):
        for z in range(2):
            rows = pl.ds(z * B, B)
            total = (
                projected[0, table[5 * size_x + z, a], rows, :]
                + projected[1, table[5 * size_x + 2 + z, a], rows, :]
            )
            csend[a, rows, :] = total.astype(BF16)
        for other_d in range(2):
            r, copy = to_coarse(a, other_d)

            @pl.when(r != 0)
            def _(copy=copy):
                copy.start()
        return carry

    lax.fori_loop(0, size_x, group_column, 0)
    cres[depth, lateral] = csend[lateral]

    clear(cpad, *[(dx, every, y) for dx in range(3) for y in (0, size_l + 1)])
    for index in range(2):
        @pl.when(jnp.logical_not(sides[index][1]))
        def _(index=index):
            clear(cpad, 2 * index)

    for load in loads[9:]:
        load.wait()

    def widen(slot, carry):
        spread[slot] = cblk[slot].astype(F32)
        return carry

    lax.fori_loop(0, CODES, widen, 0)

    def sort_coarse(y, carry):
        for near in range(9):
            parts = []
            for z in range(2):
                slot = table[4 * size_x + y, near * 3 + 1 + z - depth]
                parts.append(spread[slot, pl.ds(y, H, stride=size_x), :])
            even, odd = even_odd(low[:H], *parts)
            at = pl.ds(near * 128, 128)
            coarse[y, pl.ds(0, H), at] = even.astype(BF16)
            coarse[y, pl.ds(H, H), at] = odd.astype(BF16)
        chosen = lax.broadcasted_iota(jnp.int32, (size_x, B), 0) == y
        mass = jnp.where(chosen, cmass[...].astype(F32), 0.0)
        mass = jnp.sum(mass, axis=0, keepdims=True)
        mass = jnp.broadcast_to(jnp.concatenate([mass, mass], axis=1), (B, 128))
        wanted = coarse_order(row[:B]) + depth * B
        coarse[y, :, pl.ds(9 * 128, 128)] = jnp.where(wanted == col[:B], mass, 0.0).astype(BF16)
        return carry

    lax.fori_loop(0, size_x, sort_coarse, 0)

    def sent_column(x, carry):
        for sweep in range(SWEEPS + 1):
            lateral_do("wait_send", sweep, x)
        return carry

    lax.fori_loop(0, size_x, sent_column, 0)
    for sweep in range(SWEEPS + 1):
        for side in range(2):
            track_do("wait_send", sweep, side)
    partner.wait()

    def from_fine(y, h):
        r = lax.rem(me - 2 * y - h + group, group)

        @pl.when(r != 0)
        def _():
            pltpu.make_async_remote_copy(
                src_ref=csend.at[y],
                dst_ref=cres.at[h, y],
                send_sem=to_send.at[r],
                recv_sem=to_recv.at[r],
                device_id=(track, y, h),
                device_id_type=MESH,
            ).wait_recv()

    def first_pair(h, pair):
        for k in range(2):
            from_fine(2 * pair + k, h)
        for z in range(2):
            rows = pl.ds(z * B, B)
            stack = [cres[h, 2 * pair + k, rows, :] for k in range(2)]
            block = call[z, pair]
            zero = jnp.zeros_like(block)
            left = jnp.concatenate(
                [jnp.where(low, block, zero), jnp.where(low, zero, block)], axis=0
            )
            value = DAMPING * dot(left, jnp.concatenate(stack, axis=0))
            plain = exact_dot(order, value.astype(BF16))
            for k in range(2):
                first[z, h, 2 * pair + k] = value[k * B : (k + 1) * B]
                cpad[1, h, 2 * pair + k + 1, rows, :] = plain[k * B : (k + 1) * B]

    def side_copy(index, h, pair):
        rows = pl.ds(2 * pair + 1, 2)
        return pltpu.make_async_remote_copy(
            src_ref=cpad.at[1, h, rows],
            dst_ref=cpad.at[2 - 2 * index, h, rows],
            send_sem=side_send.at[index, h, pair],
            recv_sem=side_recv.at[index, h, pair],
            device_id=sides[index][0],
            device_id_type=MESH,
        )

    halves = (depth, 1 - depth)
    for h in halves:
        for pair in range(pairs):
            first_pair(h, pair)
            for index in range(2):
                @pl.when(sides[index][1])
                def _(index=index, h=h, pair=pair):
                    side_copy(index, h, pair).start()

    own_rows = pl.ds(pl.multiple_of(depth * B, B), B)

    def to_fine(y, h):
        r = lax.rem(2 * y + h - me + group, group)
        return r, pltpu.make_async_remote_copy(
            src_ref=csend_back.at[h, y],
            dst_ref=corr.at[depth, lateral],
            send_sem=back_send.at[r],
            recv_sem=back_recv.at[r],
            device_id=(track, y, h),
            device_id_type=MESH,
        )

    def await_side(h, pair):
        for index in range(2):
            @pl.when(sides[1 - index][1])
            def _(index=index):
                side_copy(index, h, pair).wait_recv()

    for h in halves:
        await_side(h, 0)
        for pair in range(pairs):
            if pair + 1 < pairs:
                await_side(h, pair + 1)
            ys = (2 * pair, 2 * pair + 1)
            remain = []
            for y in ys:
                pieces = [cpad[dx, h, pl.ds(y, 3)].reshape(3 * 128, LD) for dx in range(3)]
                pieces.append(cpad[1, h, y + 1])
                total = dot(coarse[y], jnp.concatenate(pieces, axis=0))
                remain.append((cres[h, y, own_rows, :].astype(F32) - total).astype(BF16))
            block = call[depth, pair]
            zero = jnp.zeros_like(block)
            left = jnp.concatenate(
                [jnp.where(low, block, zero), jnp.where(low, zero, block)], axis=0
            )
            delta = DAMPING * dot(left, jnp.concatenate(remain, axis=0))
            for k, y in enumerate(ys):
                new = first[depth, h, y] + delta[k * B : (k + 1) * B]
                csend_back[h, y] = new.astype(BF16)
                r, copy = to_fine(y, h)

                @pl.when(r != 0)
                def _(copy=copy):
                    copy.start()

    corr[depth, lateral] = csend_back[depth, lateral]

    for index in range(2):
        for h in range(2):
            for pair in range(pairs):
                @pl.when(sides[index][1])
                def _(index=index, h=h, pair=pair):
                    side_copy(index, h, pair).wait_send()

    def sent_coarse(y, carry):
        for h in range(2):
            r, copy = to_coarse(y, h)

            @pl.when(r != 0)
            def _(copy=copy):
                copy.wait_send()
        return carry

    lax.fori_loop(0, size_l, sent_coarse, 0)

    def from_coarse(x, carry):
        for z in range(2):
            r = lax.rem(me - 2 * x - z + group, group)

            @pl.when(r != 0)
            def _(z=z, r=r):
                pltpu.make_async_remote_copy(
                    src_ref=csend_back.at[z, x],
                    dst_ref=corr.at[z, x],
                    send_sem=back_send.at[r],
                    recv_sem=back_recv.at[r],
                    device_id=(track, x, z),
                    device_id_type=MESH,
                ).wait_recv()
        return carry

    lax.fori_loop(0, size_x, from_coarse, 0)

    def final_column(x, carry):
        for y in range(2):
            parts = [
                corr[z, table[5 * size_x + 4 + 2 * y + z, x]] for z in range(2)
            ]
            iterate[x, y] += dot(transfer[2 * x + y], jnp.concatenate(parts, axis=0))
            for z in range(2):
                for parity in range(2):
                    rows = every_second(parity * B + z)
                    out[x, y, z, every_second(parity), :] = iterate[x, y, rows, :]
        return carry

    lax.fori_loop(0, size_x, final_column, 0)

    def sent_fine(y, carry):
        for h in range(2):
            r, copy = to_fine(y, h)

            @pl.when(r != 0)
            def _(copy=copy):
                copy.wait_send()
        return carry

    lax.fori_loop(0, size_l, sent_fine, 0)


def run_cycle(
    tracks, rhs, start, fine_blocks, fine_cols, fine_mass, fine_smoother, transfer, aggregate,
    coarse_blocks, coarse_cols, coarse_mass, coarse_smoother,
):
    size_x = rhs.shape[0]
    count = 2 * size_x
    group = 2 * size_x
    tiles = B * B // 128
    fine_blocks = fine_blocks.reshape(size_x, 2, 2, CODES, tiles, 128)
    fine_blocks = jnp.transpose(fine_blocks, (0, 1, 3, 4, 2, 5)).reshape(count, CODES, B, 128)
    pair = []
    for array in (fine_smoother, transfer):
        array = jnp.transpose(array.reshape(size_x, 2, 2, tiles, 128), (0, 1, 3, 2, 4))
        pair.append(array.reshape(count, B, 128))
    coarse_blocks = coarse_blocks.reshape(size_x, CODES, tiles, 128)
    coarse_blocks = jnp.transpose(coarse_blocks, (1, 2, 0, 3)).reshape(CODES, tiles * size_x, 128)
    coarse_smoother = jnp.transpose(coarse_smoother.reshape(size_x, tiles, 128), (1, 0, 2))
    coarse_smoother = coarse_smoother.reshape(tiles * size_x, 128)
    operands = (
        rhs, start, fine_blocks, fine_cols.reshape(2 * count, CODES), fine_mass, *pair,
        jnp.transpose(aggregate, (1, 2, 0)).reshape(4, size_x), coarse_blocks,
        coarse_cols.reshape(size_x, CODES), coarse_mass.reshape(size_x, B), coarse_smoother,
    )
    vmem, dma = pltpu.VMEM, pltpu.SemaphoreType.DMA
    table_rows = 5 * size_x + 8
    pairs = size_x // 2
    return pl.pallas_call(
        functools.partial(cycle_kernel, tracks),
        in_specs=[pl.BlockSpec(memory_space=pl.ANY)] * len(operands),
        out_specs=pl.BlockSpec(memory_space=pltpu.VMEM),
        out_shape=jax.ShapeDtypeStruct(rhs.shape, F32),
        scratch_shapes=[vmem(array.shape, array.dtype) for array in operands] + [
            vmem((table_rows, 128), jnp.int32),
            pltpu.SMEM((table_rows, 128), jnp.int32),
            vmem((count, 128, WIDE), BF16),
            vmem((count, 128, 128), BF16),
            vmem((count, 128, 128), BF16),
            vmem((size_x, B, WIDE), BF16),
            vmem((CODES + 1, tiles * size_x, 128), F32),
            vmem((SWEEPS + 1, size_x + 2, 4, 128, LD), BF16),
            vmem((size_x, 2, 128, LD), F32),
            vmem((size_x, 2, 128, LD), F32),
            vmem((2, size_x, 128, LD), F32),
            vmem((size_x, 128, LD), BF16),
            vmem((2, size_x, 128, LD), BF16),
            vmem((3, 2, size_x + 2, 128, LD), BF16),
            vmem((2, size_x // 2, B, 128), BF16),
            vmem((2, 2, size_x, B, LD), F32),
            vmem((2, size_x, B, LD), BF16),
            vmem((2, size_x, B, LD), BF16),
            dma((11,)), dma((count,)), dma,
            dma((SWEEPS + 1, 2, size_x)), dma((SWEEPS + 1, 2, size_x)),
            dma((SWEEPS + 1, 2, 3)), dma((SWEEPS + 1, 2, 3)),
            dma((group,)), dma((group,)), dma((group,)), dma((group,)),
            dma((2, 2, pairs)), dma((2, 2, pairs)), dma, dma,
        ],
        compiler_params=pltpu.CompilerParams(
            collective_id=0, has_side_effects=True, vmem_limit_bytes=56 << 20
        ),
        name="cycle",
    )(*operands)


def solution(mesh):
    tracks = mesh.shape["track"]

    def per_device(*arrays):
        return run_cycle(tracks, *arrays)

    in_specs = (
        P("track", "lateral", None, None, "depth"),
        P("track", "lateral", None, None, "depth"),
        P("track", "lateral", None, None, None),
        P("track", "lateral", None, None),
        P("track", "lateral", None, None),
        P("track", "lateral", None, None),
        P("track", "lateral", None, None),
        P("track", "lateral", None),
        P(("track", "lateral"), None, "depth", None, None),
        P(("track", "lateral"), None, "depth", None),
        P(("track", "lateral"), None, "depth", None),
        P(("track", "lateral"), None, "depth", None),
    )
    out_specs = P("track", "lateral", None, None, "depth")
    return jax.shard_map(
        per_device, mesh=mesh, in_specs=in_specs, out_specs=out_specs, check_vma=False
    )
```

```python
import functools

import jax
import jax.numpy as jnp
from jax import lax
from jax.experimental import pallas as pl
from jax.experimental.pallas import tpu as pltpu
from jax.sharding import PartitionSpec as P

SWEEPS = 2
DAMPING = 0.8
B = 64
H = B // 2
CODES = 27
LD = 128
WIDE = 10 * 128
F32 = jnp.float32
BF16 = jnp.bfloat16
MESH = pl.DeviceIdType.MESH


def lanes_low(rows):
    return lax.broadcasted_iota(jnp.int32, (rows, 128), 1) < B


def half_swap(block):
    return jnp.concatenate([block[:, B:], block[:, :B]], axis=1)


def even_odd(low, first, second):
    return jnp.where(low, first, half_swap(second)), jnp.where(low, half_swap(first), second)


def fine_order(index):
    return index % 2 * B + index % B // 2 * 2 + index // B


def coarse_order(index):
    return index // B * B + index % H * 2 + index % B // H


def order_matrix(order):
    row = lax.broadcasted_iota(jnp.int32, (128, 128), 0)
    col = lax.broadcasted_iota(jnp.int32, (128, 128), 1)
    return (row == order(col)).astype(F32).astype(BF16)


def exact_dot(left, right):
    return dot(left, right).astype(BF16)


def dot(left, right):
    return jnp.dot(left, right, preferred_element_type=F32)


def every_second(parity):
    return pl.ds(parity, H, stride=2)


def inverse_rows(lists, count):
    rows = lists.shape[0]
    lane = lax.broadcasted_iota(jnp.int32, (rows, 128), 1)
    found = jnp.zeros((rows, 128), jnp.int32)
    for k in range(count):
        found = jnp.where(lists[:, k : k + 1] == lane, k, found)
    return found


def cycle_kernel(
    tracks,
    rhs_hbm, start_hbm, fblk_hbm, fcols_hbm, fmass_hbm, fsm_hbm, tran_hbm, agg_hbm,
    cblk_hbm, ccols_hbm, cmass_hbm, csm_hbm,
    out,
    rhs, start, fblk, fcols, fmass, fsm, tran, agg, cblk, ccols, cmass, csm,
    rows_table, table, fine, smooth, transfer, coarse, spread,
    padded, forces, iterate, projected, csend, cres, cpad, call, first, csend_back, corr,
    load_sem, block_sem, table_sem,
    lat_send, lat_recv, track_send, track_recv,
    to_send, to_recv, back_send, back_recv, side_send, side_recv, ss_send, ss_recv, ready,
):
    size_x = rhs.shape[0]
    size_l = size_x
    count = 2 * size_x
    group = 2 * size_l
    last = size_x - 1
    track = lax.axis_index("track")
    lateral = lax.axis_index("lateral")
    depth = lax.axis_index("depth")
    me = lateral * 2 + depth

    def exists(dt, dl):
        ok = None
        for step, at, ends in ((dt, track, tracks), (dl, lateral, size_l)):
            if step:
                here = (at > 0) if step < 0 else (at < ends - 1)
                ok = here if ok is None else jnp.logical_and(ok, here)
        return ok

    at_first = (lateral == 0).astype(jnp.int32)
    at_last = (lateral == last).astype(jnp.int32)
    before = (track - at_first, lax.rem(lateral + last, size_l), lax.rem(depth + at_first, 2))
    after = (track + at_last, lax.rem(lateral + 1, size_l), lax.rem(depth + at_last, 2))
    sides = (
        (before, jnp.logical_or(track > 0, lateral > 0)),
        (after, jnp.logical_or(track < tracks - 1, lateral < last)),
    )

    barrier = pltpu.get_barrier_semaphore()
    upper_depth = (depth == 1).astype(jnp.int32)

    def greet(device, ok):
        @pl.when(ok)
        def _():
            pl.semaphore_signal(barrier, inc=1, device_id=device, device_id_type=MESH)

    expected = size_l - 1 + upper_depth * size_l
    for r in range(1, size_l):
        greet((track, lax.rem(lateral + r, size_l), depth), True)
    for r in range(size_l):
        greet((track, r, 1), depth == 0)
    for dt in (-1, 1):
        for dl in (-1, 0, 1):
            ok = exists(dt, dl)
            greet((track + dt, lateral + dl, depth), ok)
            expected = expected + ok.astype(jnp.int32)
    crossings = [
        jnp.logical_and(ok, at_end)
        for (_, ok), at_end in zip(sides, (lateral == 0, lateral == last))
    ]
    crossing_count = sum(crossing.astype(jnp.int32) for crossing in crossings)
    for (device, _), crossing in zip(sides, crossings):
        greet(device, jnp.logical_and(crossing, depth == 0))
    expected = expected + upper_depth * crossing_count

    small = [
        (start_hbm, start), (fcols_hbm, fcols), (ccols_hbm, ccols), (agg_hbm, agg),
        (fmass_hbm, fmass), (fsm_hbm, fsm), (tran_hbm, tran), (rhs_hbm, rhs),
        (csm_hbm, csm), (cmass_hbm, cmass), (cblk_hbm, cblk),
    ]
    loads = [
        pltpu.make_async_copy(source, target, load_sem.at[k])
        for k, (source, target) in enumerate(small)
    ]

    def block_load(i):
        return pltpu.make_async_copy(fblk_hbm.at[i], fblk.at[i], block_sem.at[i])

    for load in loads[:8]:
        load.start()

    def start_block(i, carry):
        block_load(i).start()
        return carry

    lax.fori_loop(0, count, start_block, 0)
    for load in loads[8:]:
        load.start()

    def clear(ref, *places):
        for place in places:
            ref[place] = jnp.zeros_like(ref[place])

    every = slice(None)
    for missing, place in (
        (track == 0, (0,)), (track == tracks - 1, (size_x + 1,)),
        (lateral == 0, (every, 0)), (lateral == last, (every, 3)),
    ):
        @pl.when(missing)
        def _(place=place):
            clear(padded, *[(sweep,) + place for sweep in range(SWEEPS + 1)])

    def round_start(x, carry):
        for y in range(2):
            for z in range(2):
                padded[0, x + 1, y + 1, pl.ds(z * B, B), :] = start[x, y, z].astype(BF16)
        return carry

    loads[0].wait()
    lax.fori_loop(0, size_x, round_start, 0)
    pl.semaphore_wait(barrier, expected)

    @pl.when(depth == 1)
    def _():
        for r in range(size_l):
            pl.semaphore_signal(ready, inc=1, device_id=(track, r, 0), device_id_type=MESH)
        for (device, _), crossing in zip(sides, crossings):
            @pl.when(crossing)
            def _(device=device):
                pl.semaphore_signal(ready, inc=1, device_id=device, device_id_type=MESH)

    def lateral_copy(sweep, x, side):
        columns = x + 1
        return pltpu.make_async_remote_copy(
            src_ref=padded.at[sweep, columns, 1 + side],
            dst_ref=padded.at[sweep, columns, 3 - 3 * side],
            send_sem=lat_send.at[sweep, side, x],
            recv_sem=lat_recv.at[sweep, side, x],
            device_id=(track, lateral + 2 * side - 1, depth),
            device_id_type=MESH,
        )

    def track_copy(sweep, side, dl):
        src_y, dst_y = {0: (pl.ds(1, 2),) * 2, -1: (1, 3), 1: (2, 0)}[dl]
        return pltpu.make_async_remote_copy(
            src_ref=padded.at[sweep, size_x if side else 1, src_y],
            dst_ref=padded.at[sweep, 0 if side else size_x + 1, dst_y],
            send_sem=track_send.at[sweep, side, dl + 1],
            recv_sem=track_recv.at[sweep, side, dl + 1],
            device_id=(track + 2 * side - 1, lateral + dl, depth),
            device_id_type=MESH,
        )

    def lateral_do(action, sweep, x):
        for side in range(2):
            step = 2 * side - 1

            @pl.when(exists(0, -step if action == "wait_recv" else step))
            def _(side=side):
                getattr(lateral_copy(sweep, x, side), action)()

    def track_do(action, sweep, side):
        step = 2 * side - 1
        for dl in (0, -1, 1):
            here = (-step, -dl) if action == "wait_recv" else (step, dl)

            @pl.when(exists(*here))
            def _(dl=dl):
                getattr(track_copy(sweep, side, dl), action)()

    pairs = size_x // 2
    in_order = [(x, x + 1) for x in range(0, size_x, 2)]
    ends_paired = [(0, last)] + [(x, x + 1) for x in range(1, last, 2)]
    outer_first = list(dict.fromkeys([in_order[0], in_order[-1]] + in_order))
    passes = (outer_first, ends_paired, in_order)
    ahead = {}
    for sweep, sequence in enumerate(passes):
        known = set()
        for xs in sequence:
            wanted = sorted({x + k for x in xs for k in (-1, 0, 1) if 0 <= x + k <= last})
            ahead[sweep, xs] = [x for x in wanted if x not in known]
            known.update(wanted)

    for side in range(2):
        track_do("start", 0, side)
    for xs in outer_first:
        for x in ahead[0, xs]:
            lateral_do("start", 0, x)

    for load in loads[1:4]:
        load.wait()
    rows_table[pl.ds(0, 4 * size_x), :] = inverse_rows(fcols[...], CODES)
    rows_table[pl.ds(4 * size_x, size_x), :] = inverse_rows(ccols[...], CODES)
    groups = lax.rem(agg[...], size_x)
    rows_table[pl.ds(5 * size_x, 4), :] = inverse_rows(groups, size_x)
    rows_table[pl.ds(5 * size_x + 4, 4), pl.ds(0, size_x)] = groups
    fill = pltpu.make_async_copy(rows_table, table, table_sem)
    fill.start()
    for load in loads[4:9]:
        load.wait()

    def reorder(x, carry):
        for y in range(2):
            for z in range(2):
                for parity in range(2):
                    rows = every_second(parity * B + z)
                    for source, target in ((rhs, forces), (start, iterate)):
                        target[x, y, rows, :] = source[x, y, z, every_second(parity), :]
        return carry

    lax.fori_loop(0, size_x, reorder, 0)
    swap = order_matrix(fine_order)
    order = order_matrix(coarse_order)
    low = lanes_low(B)
    upper = lax.broadcasted_iota(jnp.int32, (B, 128), 0) % 2 == 0
    row = lax.broadcasted_iota(jnp.int32, (128, 128), 0)
    col = lax.broadcasted_iota(jnp.int32, (128, 128), 1)

    spread[CODES] = csm[...].astype(F32)
    for pair in range(size_x // 2):
        parts = [spread[CODES, pl.ds(2 * pair + k, H, stride=size_x), :] for k in range(2)]
        even, odd = even_odd(low[:H], *parts)
        both = jnp.concatenate([even, odd], axis=0).astype(BF16)
        call[depth, pair] = exact_dot(both, order)
    partner = pltpu.make_async_remote_copy(
        src_ref=call.at[depth],
        dst_ref=call.at[depth],
        send_sem=ss_send,
        recv_sem=ss_recv,
        device_id=(track, lateral, 1 - depth),
        device_id_type=MESH,
    )
    fill.wait()

    def wait_block(i, carry):
        block_load(i).wait()
        return carry

    lax.fori_loop(0, count, wait_block, 0)

    def sort_fine(i, carry):
        def block(layer, code):
            return fblk[i, table[2 * i + layer, code]]

        for near in range(9):
            code = near * 3 + 1
            one = jnp.where(upper, block(0, code), block(1, code - 1))
            two = jnp.where(upper, block(0, code + 1), block(1, code))
            even, odd = even_odd(low, one, two)
            at = pl.ds(near * 128, 128)
            fine[i, pl.ds(0, B), at] = even
            fine[i, pl.ds(B, B), at] = odd
        mass = fmass[i // 2, lax.rem(i, 2)].astype(F32)
        mass = jnp.concatenate([mass[0:1], mass[1:2]], axis=1)
        diag = jnp.where(fine_order(row) == col, jnp.broadcast_to(mass, (128, 128)), 0.0)
        fine[i, :, pl.ds(9 * 128, 128)] = diag.astype(BF16)
        for source, target, reordering in ((fsm, smooth, swap), (tran, transfer, order)):
            whole = source[i]
            zero = jnp.zeros_like(whole)
            even, odd = even_odd(low, jnp.where(upper, whole, zero), jnp.where(upper, zero, whole))
            target[i] = exact_dot(jnp.concatenate([even, odd], axis=0), reordering)
        return carry

    lax.fori_loop(0, count, sort_fine, 0)
    def apply_fine(sweep, x, y):
        pieces = [
            padded[sweep, x + dx, pl.ds(y, 3)].reshape(3 * 128, LD) for dx in range(3)
        ]
        pieces.append(padded[sweep, x + 1, y + 1])
        return dot(fine[2 * x + y], jnp.concatenate(pieces, axis=0))

    def await_halo(sweep, xs):
        if 0 in xs:
            track_do("wait_recv", sweep, 1)
        if last in xs:
            track_do("wait_recv", sweep, 0)
        for x in ahead[sweep, xs]:
            lateral_do("wait_recv", sweep, x)

    def residuals(sweep, cells):
        totals = [apply_fine(sweep, x, y) for x, y in cells]
        return [(forces[x, y] - t).astype(BF16) for (x, y), t in zip(cells, totals)]

    for sweep in range(SWEEPS):
        for xs in passes[sweep]:
            await_halo(sweep, xs)
            if sweep == 0 and xs == passes[0][-1]:
                pl.when(depth == 1)(partner.start)
            cells = [(x, y) for x in xs for y in range(2)]
            res = residuals(sweep, cells)
            steps = [DAMPING * dot(smooth[2 * x + y], r) for (x, y), r in zip(cells, res)]
            news = [iterate[x, y] + step for (x, y), step in zip(cells, steps)]
            plain = [exact_dot(swap, new.astype(BF16)) for new in news]
            for (x, y), new, rounded in zip(cells, news, plain):
                iterate[x, y] = new
                padded[sweep + 1, x + 1, y + 1] = rounded
            if 0 in xs:
                track_do("start", sweep + 1, 0)
            if last in xs:
                track_do("start", sweep + 1, 1)
            for x in xs:
                lateral_do("start", sweep + 1, x)

    for xs in passes[SWEEPS]:
        await_halo(SWEEPS, xs)
        cells = [(x, y) for x in xs for y in range(2)]
        for (x, y), r in zip(cells, residuals(SWEEPS, cells)):
            projected[y, x] = lax.dot_general(
                transfer[2 * x + y], r, (((0,), (0,)), ((), ())), preferred_element_type=F32
            )

    @pl.when(depth == 0)
    def _():
        pl.semaphore_wait(ready, size_l + crossing_count)
        partner.start()

    def to_coarse(other_l, other_d):
        r = lax.rem(other_l * 2 + other_d - me + group, group)
        return r, pltpu.make_async_remote_copy(
            src_ref=csend.at[other_l],
            dst_ref=cres.at[depth, lateral],
            send_sem=to_send.at[r],
            recv_sem=to_recv.at[r],
            device_id=(track, other_l, other_d),
            device_id_type=MESH,
        )

    def group_column(i, carry):
        a = lax.rem(lateral + 1 + i, size_x)
        for z in range(2):
            rows = pl.ds(z * B, B)
            total = (
                projected[0, table[5 * size_x + z, a], rows, :]
                + projected[1, table[5 * size_x + 2 + z, a], rows, :]
            )
            csend[a, rows, :] = total.astype(BF16)
        for other_d in range(2):
            r, copy = to_coarse(a, other_d)

            @pl.when(r != 0)
            def _(copy=copy):
                copy.start()
        return carry

    lax.fori_loop(0, size_x, group_column, 0)
    cres[depth, lateral] = csend[lateral]

    clear(cpad, *[(dx, every, y) for dx in range(3) for y in (0, size_l + 1)])
    for index in range(2):
        @pl.when(jnp.logical_not(sides[index][1]))
        def _(index=index):
            clear(cpad, 2 * index)

    def from_fine(y, h):
        r = lax.rem(me - 2 * y - h + group, group)

        @pl.when(r != 0)
        def _():
            pltpu.make_async_remote_copy(
                src_ref=csend.at[y],
                dst_ref=cres.at[h, y],
                send_sem=to_send.at[r],
                recv_sem=to_recv.at[r],
                device_id=(track, y, h),
                device_id_type=MESH,
            ).wait_recv()

    def first_pair(h, pair):
        for k in range(2):
            from_fine(2 * pair + k, h)
        for z in range(2):
            rows = pl.ds(z * B, B)
            stack = [cres[h, 2 * pair + k, rows, :] for k in range(2)]
            block = call[z, pair]
            zero = jnp.zeros_like(block)
            left = jnp.concatenate(
                [jnp.where(low, block, zero), jnp.where(low, zero, block)], axis=0
            )
            value = DAMPING * dot(left, jnp.concatenate(stack, axis=0))
            plain = exact_dot(order, value.astype(BF16))
            for k in range(2):
                first[z, h, 2 * pair + k] = value[k * B : (k + 1) * B]
                cpad[1, h, 2 * pair + k + 1, rows, :] = plain[k * B : (k + 1) * B]

    def side_copy(index, h, pair):
        rows = pl.ds(2 * pair + 1, 2)
        return pltpu.make_async_remote_copy(
            src_ref=cpad.at[1, h, rows],
            dst_ref=cpad.at[2 - 2 * index, h, rows],
            send_sem=side_send.at[index, h, pair],
            recv_sem=side_recv.at[index, h, pair],
            device_id=sides[index][0],
            device_id_type=MESH,
        )

    def first_half(h):
        for pair in range(pairs):
            first_pair(h, pair)
            for index in range(2):
                @pl.when(sides[index][1])
                def _(index=index, pair=pair):
                    side_copy(index, h, pair).start()

    partner.wait()
    first_half(0)

    for load in loads[9:]:
        load.wait()

    def widen(slot, carry):
        spread[slot] = cblk[slot].astype(F32)
        return carry

    lax.fori_loop(0, CODES, widen, 0)

    def sort_coarse(y, carry):
        for near in range(9):
            parts = []
            for z in range(2):
                slot = table[4 * size_x + y, near * 3 + 1 + z - depth]
                parts.append(spread[slot, pl.ds(y, H, stride=size_x), :])
            even, odd = even_odd(low[:H], *parts)
            at = pl.ds(near * 128, 128)
            coarse[y, pl.ds(0, H), at] = even.astype(BF16)
            coarse[y, pl.ds(H, H), at] = odd.astype(BF16)
        chosen = lax.broadcasted_iota(jnp.int32, (size_x, B), 0) == y
        mass = jnp.where(chosen, cmass[...].astype(F32), 0.0)
        mass = jnp.sum(mass, axis=0, keepdims=True)
        mass = jnp.broadcast_to(jnp.concatenate([mass, mass], axis=1), (B, 128))
        wanted = coarse_order(row[:B]) + depth * B
        coarse[y, :, pl.ds(9 * 128, 128)] = jnp.where(wanted == col[:B], mass, 0.0).astype(BF16)
        return carry

    lax.fori_loop(0, size_x, sort_coarse, 0)

    first_half(1)
    def sent_column(x, carry):
        for sweep in range(SWEEPS + 1):
            lateral_do("wait_send", sweep, x)
        return carry

    lax.fori_loop(0, size_x, sent_column, 0)
    for sweep in range(SWEEPS + 1):
        for side in range(2):
            track_do("wait_send", sweep, side)


    own_rows = pl.ds(pl.multiple_of(depth * B, B), B)

    def to_fine(y, h):
        r = lax.rem(2 * y + h - me + group, group)
        return r, pltpu.make_async_remote_copy(
            src_ref=csend_back.at[h, y],
            dst_ref=corr.at[depth, lateral],
            send_sem=back_send.at[r],
            recv_sem=back_recv.at[r],
            device_id=(track, y, h),
            device_id_type=MESH,
        )

    def await_side(h, pair):
        for index in range(2):
            @pl.when(sides[1 - index][1])
            def _(index=index):
                side_copy(index, h, pair).wait_recv()

    for h in range(2):
        await_side(h, 0)
        for pair in range(pairs):
            if pair + 1 < pairs:
                await_side(h, pair + 1)
            ys = (2 * pair, 2 * pair + 1)
            remain = []
            for y in ys:
                pieces = [cpad[dx, h, pl.ds(y, 3)].reshape(3 * 128, LD) for dx in range(3)]
                pieces.append(cpad[1, h, y + 1])
                total = dot(coarse[y], jnp.concatenate(pieces, axis=0))
                remain.append((cres[h, y, own_rows, :].astype(F32) - total).astype(BF16))
            block = call[depth, pair]
            zero = jnp.zeros_like(block)
            left = jnp.concatenate(
                [jnp.where(low, block, zero), jnp.where(low, zero, block)], axis=0
            )
            delta = DAMPING * dot(left, jnp.concatenate(remain, axis=0))
            for k, y in enumerate(ys):
                new = first[depth, h, y] + delta[k * B : (k + 1) * B]
                csend_back[h, y] = new.astype(BF16)
                r, copy = to_fine(y, h)

                @pl.when(r != 0)
                def _(copy=copy):
                    copy.start()

    corr[depth, lateral] = csend_back[depth, lateral]

    for index in range(2):
        for h in range(2):
            for pair in range(pairs):
                @pl.when(sides[index][1])
                def _(index=index, h=h, pair=pair):
                    side_copy(index, h, pair).wait_send()

    def sent_coarse(y, carry):
        for h in range(2):
            r, copy = to_coarse(y, h)

            @pl.when(r != 0)
            def _(copy=copy):
                copy.wait_send()
        return carry

    lax.fori_loop(0, size_l, sent_coarse, 0)

    def from_coarse(x, carry):
        for z in range(2):
            r = lax.rem(me - 2 * x - z + group, group)

            @pl.when(r != 0)
            def _(z=z, r=r):
                pltpu.make_async_remote_copy(
                    src_ref=csend_back.at[z, x],
                    dst_ref=corr.at[z, x],
                    send_sem=back_send.at[r],
                    recv_sem=back_recv.at[r],
                    device_id=(track, x, z),
                    device_id_type=MESH,
                ).wait_recv()
        return carry

    lax.fori_loop(0, size_x, from_coarse, 0)

    def final_column(x, carry):
        for y in range(2):
            parts = [
                corr[z, table[5 * size_x + 4 + 2 * y + z, x]] for z in range(2)
            ]
            iterate[x, y] += dot(transfer[2 * x + y], jnp.concatenate(parts, axis=0))
            for z in range(2):
                for parity in range(2):
                    rows = every_second(parity * B + z)
                    out[x, y, z, every_second(parity), :] = iterate[x, y, rows, :]
        return carry

    lax.fori_loop(0, size_x, final_column, 0)

    def sent_fine(y, carry):
        for h in range(2):
            r, copy = to_fine(y, h)

            @pl.when(r != 0)
            def _(copy=copy):
                copy.wait_send()
        return carry

    lax.fori_loop(0, size_l, sent_fine, 0)


def run_cycle(
    tracks, rhs, start, fine_blocks, fine_cols, fine_mass, fine_smoother, transfer, aggregate,
    coarse_blocks, coarse_cols, coarse_mass, coarse_smoother,
):
    size_x = rhs.shape[0]
    count = 2 * size_x
    group = 2 * size_x
    tiles = B * B // 128
    fine_blocks = fine_blocks.reshape(size_x, 2, 2, CODES, tiles, 128)
    fine_blocks = jnp.transpose(fine_blocks, (0, 1, 3, 4, 2, 5)).reshape(count, CODES, B, 128)
    pair = []
    for array in (fine_smoother, transfer):
        array = jnp.transpose(array.reshape(size_x, 2, 2, tiles, 128), (0, 1, 3, 2, 4))
        pair.append(array.reshape(count, B, 128))
    coarse_blocks = coarse_blocks.reshape(size_x, CODES, tiles, 128)
    coarse_blocks = jnp.transpose(coarse_blocks, (1, 2, 0, 3)).reshape(CODES, tiles * size_x, 128)
    coarse_smoother = jnp.transpose(coarse_smoother.reshape(size_x, tiles, 128), (1, 0, 2))
    coarse_smoother = coarse_smoother.reshape(tiles * size_x, 128)
    operands = (
        rhs, start, fine_blocks, fine_cols.reshape(2 * count, CODES), fine_mass, *pair,
        jnp.transpose(aggregate, (1, 2, 0)).reshape(4, size_x), coarse_blocks,
        coarse_cols.reshape(size_x, CODES), coarse_mass.reshape(size_x, B), coarse_smoother,
    )
    vmem, dma = pltpu.VMEM, pltpu.SemaphoreType.DMA
    table_rows = 5 * size_x + 8
    pairs = size_x // 2
    return pl.pallas_call(
        functools.partial(cycle_kernel, tracks),
        in_specs=[pl.BlockSpec(memory_space=pl.ANY)] * len(operands),
        out_specs=pl.BlockSpec(memory_space=pltpu.VMEM),
        out_shape=jax.ShapeDtypeStruct(rhs.shape, F32),
        scratch_shapes=[vmem(array.shape, array.dtype) for array in operands] + [
            vmem((table_rows, 128), jnp.int32),
            pltpu.SMEM((table_rows, 128), jnp.int32),
            vmem((count, 128, WIDE), BF16),
            vmem((count, 128, 128), BF16),
            vmem((count, 128, 128), BF16),
            vmem((size_x, B, WIDE), BF16),
            vmem((CODES + 1, tiles * size_x, 128), F32),
            vmem((SWEEPS + 1, size_x + 2, 4, 128, LD), BF16),
            vmem((size_x, 2, 128, LD), F32),
            vmem((size_x, 2, 128, LD), F32),
            vmem((2, size_x, 128, LD), F32),
            vmem((size_x, 128, LD), BF16),
            vmem((2, size_x, 128, LD), BF16),
            vmem((3, 2, size_x + 2, 128, LD), BF16),
            vmem((2, size_x // 2, B, 128), BF16),
            vmem((2, 2, size_x, B, LD), F32),
            vmem((2, size_x, B, LD), BF16),
            vmem((2, size_x, B, LD), BF16),
            dma((11,)), dma((count,)), dma,
            dma((SWEEPS + 1, 2, size_x)), dma((SWEEPS + 1, 2, size_x)),
            dma((SWEEPS + 1, 2, 3)), dma((SWEEPS + 1, 2, 3)),
            dma((group,)), dma((group,)), dma((group,)), dma((group,)),
            dma((2, 2, pairs)), dma((2, 2, pairs)), dma, dma,
            pltpu.SemaphoreType.REGULAR,
        ],
        compiler_params=pltpu.CompilerParams(
            collective_id=0, has_side_effects=True, vmem_limit_bytes=56 << 20
        ),
        name="cycle",
    )(*operands)


def solution(mesh):
    tracks = mesh.shape["track"]

    def per_device(*arrays):
        return run_cycle(tracks, *arrays)

    in_specs = (
        P("track", "lateral", None, None, "depth"),
        P("track", "lateral", None, None, "depth"),
        P("track", "lateral", None, None, None),
        P("track", "lateral", None, None),
        P("track", "lateral", None, None),
        P("track", "lateral", None, None),
        P("track", "lateral", None, None),
        P("track", "lateral", None),
        P(("track", "lateral"), None, "depth", None, None),
        P(("track", "lateral"), None, "depth", None),
        P(("track", "lateral"), None, "depth", None),
        P(("track", "lateral"), None, "depth", None),
    )
    out_specs = P("track", "lateral", None, None, "depth")
    return jax.shard_map(
        per_device, mesh=mesh, in_specs=in_specs, out_specs=out_specs, check_vma=False
    )
```

```python
import functools

import jax
import jax.numpy as jnp
from jax import lax
from jax.experimental import pallas as pl
from jax.experimental.pallas import tpu as pltpu
from jax.sharding import PartitionSpec as P

SWEEPS = 2
DAMPING = 0.8
B = 64
H = B // 2
CODES = 27
LD = 128
WIDE = 10 * 128
F32 = jnp.float32
BF16 = jnp.bfloat16
MESH = pl.DeviceIdType.MESH


def lanes_low(rows):
    return lax.broadcasted_iota(jnp.int32, (rows, 128), 1) < B


def half_swap(block):
    return jnp.concatenate([block[:, B:], block[:, :B]], axis=1)


def even_odd(low, first, second):
    return jnp.where(low, first, half_swap(second)), jnp.where(low, half_swap(first), second)


def fine_order(index):
    return index % 2 * B + index % B // 2 * 2 + index // B


def coarse_order(index):
    return index // B * B + index % H * 2 + index % B // H


def order_matrix(order):
    row = lax.broadcasted_iota(jnp.int32, (128, 128), 0)
    col = lax.broadcasted_iota(jnp.int32, (128, 128), 1)
    return (row == order(col)).astype(F32).astype(BF16)


def exact_dot(left, right):
    return dot(left, right).astype(BF16)


def dot(left, right):
    return jnp.dot(left, right, preferred_element_type=F32)


def every_second(parity):
    return pl.ds(parity, H, stride=2)


def inverse_rows(lists, count):
    rows = lists.shape[0]
    lane = lax.broadcasted_iota(jnp.int32, (rows, 128), 1)
    found = jnp.zeros((rows, 128), jnp.int32)
    for k in range(count):
        found = jnp.where(lists[:, k : k + 1] == lane, k, found)
    return found


def cycle_kernel(
    tracks,
    rhs_hbm, start_hbm, fblk_hbm, fcols_hbm, fmass_hbm, fsm_hbm, tran_hbm, agg_hbm,
    cblk_hbm, ccols_hbm, cmass_hbm, csm_hbm,
    out,
    rhs, start, fblk_low, fblk_high, fcols, fmass, fsm, tran, agg, cblk, ccols, cmass, csm,
    rows_table, table, fine, smooth, transfer, coarse, spread,
    padded, forces, iterate, projected, csend, cres, cpad, call, first, csend_back, corr,
    load_sem, block_sem, table_sem,
    lat_send, lat_recv, track_send, track_recv,
    to_send, to_recv, back_send, back_recv, side_send, side_recv, ss_send, ss_recv, ready,
):
    size_x = rhs.shape[0]
    size_l = size_x
    count = 2 * size_x
    group = 2 * size_l
    last = size_x - 1
    track = lax.axis_index("track")
    lateral = lax.axis_index("lateral")
    depth = lax.axis_index("depth")
    me = lateral * 2 + depth

    def exists(dt, dl):
        ok = None
        for step, at, ends in ((dt, track, tracks), (dl, lateral, size_l)):
            if step:
                here = (at > 0) if step < 0 else (at < ends - 1)
                ok = here if ok is None else jnp.logical_and(ok, here)
        return ok

    at_first = (lateral == 0).astype(jnp.int32)
    at_last = (lateral == last).astype(jnp.int32)
    before = (track - at_first, lax.rem(lateral + last, size_l), lax.rem(depth + at_first, 2))
    after = (track + at_last, lax.rem(lateral + 1, size_l), lax.rem(depth + at_last, 2))
    sides = (
        (before, jnp.logical_or(track > 0, lateral > 0)),
        (after, jnp.logical_or(track < tracks - 1, lateral < last)),
    )

    barrier = pltpu.get_barrier_semaphore()
    upper_depth = (depth == 1).astype(jnp.int32)

    def greet(device, ok):
        @pl.when(ok)
        def _():
            pl.semaphore_signal(barrier, inc=1, device_id=device, device_id_type=MESH)

    expected = size_l - 1 + upper_depth * size_l
    for r in range(1, size_l):
        greet((track, lax.rem(lateral + r, size_l), depth), True)
    for r in range(size_l):
        greet((track, r, 1), depth == 0)
    for dt in (-1, 1):
        for dl in (-1, 0, 1):
            ok = exists(dt, dl)
            greet((track + dt, lateral + dl, depth), ok)
            expected = expected + ok.astype(jnp.int32)
    crossings = [
        jnp.logical_and(ok, at_end)
        for (_, ok), at_end in zip(sides, (lateral == 0, lateral == last))
    ]
    crossing_count = sum(crossing.astype(jnp.int32) for crossing in crossings)
    for (device, _), crossing in zip(sides, crossings):
        greet(device, jnp.logical_and(crossing, depth == 0))
    expected = expected + upper_depth * crossing_count

    small = [
        (start_hbm, start), (fcols_hbm, fcols), (ccols_hbm, ccols), (agg_hbm, agg),
        (fmass_hbm, fmass), (fsm_hbm, fsm), (tran_hbm, tran), (rhs_hbm, rhs),
        (csm_hbm, csm), (cmass_hbm, cmass), (cblk_hbm, cblk),
    ]
    loads = [
        pltpu.make_async_copy(source, target, load_sem.at[k])
        for k, (source, target) in enumerate(small)
    ]

    def block_load(half, i):
        at = half * size_x + i
        return pltpu.make_async_copy(fblk_hbm.at[at], fblk[half].at[i], block_sem.at[at])

    for load in loads[:8]:
        load.start()

    fblk = (fblk_low, fblk_high)
    for half in range(2):
        def start_block(i, carry, half=half):
            block_load(half, i).start()
            return carry

        lax.fori_loop(0, size_x, start_block, 0)
    for load in loads[8:]:
        load.start()

    def clear(ref, *places):
        for place in places:
            ref[place] = jnp.zeros_like(ref[place])

    every = slice(None)
    for missing, place in (
        (track == 0, (0,)), (track == tracks - 1, (size_x + 1,)),
        (lateral == 0, (every, 0)), (lateral == last, (every, 3)),
    ):
        @pl.when(missing)
        def _(place=place):
            clear(padded, *[(sweep,) + place for sweep in range(SWEEPS + 1)])

    def round_start(x, carry):
        for y in range(2):
            for z in range(2):
                padded[0, x + 1, y + 1, pl.ds(z * B, B), :] = start[x, y, z].astype(BF16)
        return carry

    loads[0].wait()
    lax.fori_loop(0, size_x, round_start, 0)
    pl.semaphore_wait(barrier, expected)

    @pl.when(depth == 1)
    def _():
        for r in range(size_l):
            pl.semaphore_signal(ready, inc=1, device_id=(track, r, 0), device_id_type=MESH)
        for (device, _), crossing in zip(sides, crossings):
            @pl.when(crossing)
            def _(device=device):
                pl.semaphore_signal(ready, inc=1, device_id=device, device_id_type=MESH)

    def lateral_copy(sweep, x, side):
        columns = x + 1
        return pltpu.make_async_remote_copy(
            src_ref=padded.at[sweep, columns, 1 + side],
            dst_ref=padded.at[sweep, columns, 3 - 3 * side],
            send_sem=lat_send.at[sweep, side, x],
            recv_sem=lat_recv.at[sweep, side, x],
            device_id=(track, lateral + 2 * side - 1, depth),
            device_id_type=MESH,
        )

    def track_copy(sweep, side, dl):
        src_y, dst_y = {0: (pl.ds(1, 2),) * 2, -1: (1, 3), 1: (2, 0)}[dl]
        return pltpu.make_async_remote_copy(
            src_ref=padded.at[sweep, size_x if side else 1, src_y],
            dst_ref=padded.at[sweep, 0 if side else size_x + 1, dst_y],
            send_sem=track_send.at[sweep, side, dl + 1],
            recv_sem=track_recv.at[sweep, side, dl + 1],
            device_id=(track + 2 * side - 1, lateral + dl, depth),
            device_id_type=MESH,
        )

    def lateral_do(action, sweep, x):
        for side in range(2):
            step = 2 * side - 1

            @pl.when(exists(0, -step if action == "wait_recv" else step))
            def _(side=side):
                getattr(lateral_copy(sweep, x, side), action)()

    def track_do(action, sweep, side):
        step = 2 * side - 1
        for dl in (0, -1, 1):
            here = (-step, -dl) if action == "wait_recv" else (step, dl)

            @pl.when(exists(*here))
            def _(dl=dl):
                getattr(track_copy(sweep, side, dl), action)()

    pairs = size_x // 2
    in_order = [(x, x + 1) for x in range(0, size_x, 2)]
    ends_paired = [(0, last)] + [(x, x + 1) for x in range(1, last, 2)]
    outer_first = list(dict.fromkeys([in_order[0], in_order[-1]] + in_order))
    passes = (outer_first, ends_paired, in_order)
    ahead = {}
    for sweep, sequence in enumerate(passes):
        known = set()
        for xs in sequence:
            wanted = sorted({x + k for x in xs for k in (-1, 0, 1) if 0 <= x + k <= last})
            ahead[sweep, xs] = [x for x in wanted if x not in known]
            known.update(wanted)

    for side in range(2):
        track_do("start", 0, side)
    for xs in outer_first:
        for x in ahead[0, xs]:
            lateral_do("start", 0, x)

    for load in loads[1:4]:
        load.wait()
    rows_table[pl.ds(0, 4 * size_x), :] = inverse_rows(fcols[...], CODES)
    rows_table[pl.ds(4 * size_x, size_x), :] = inverse_rows(ccols[...], CODES)
    groups = lax.rem(agg[...], size_x)
    rows_table[pl.ds(5 * size_x, 4), :] = inverse_rows(groups, size_x)
    rows_table[pl.ds(5 * size_x + 4, 4), pl.ds(0, size_x)] = groups
    fill = pltpu.make_async_copy(rows_table, table, table_sem)
    fill.start()
    for load in loads[4:9]:
        load.wait()

    def reorder(x, carry):
        for y in range(2):
            for z in range(2):
                for parity in range(2):
                    rows = every_second(parity * B + z)
                    for source, target in ((rhs, forces), (start, iterate)):
                        target[x, y, rows, :] = source[x, y, z, every_second(parity), :]
        return carry

    lax.fori_loop(0, size_x, reorder, 0)
    swap = order_matrix(fine_order)
    order = order_matrix(coarse_order)
    low = lanes_low(B)
    upper = lax.broadcasted_iota(jnp.int32, (B, 128), 0) % 2 == 0
    row = lax.broadcasted_iota(jnp.int32, (128, 128), 0)
    col = lax.broadcasted_iota(jnp.int32, (128, 128), 1)

    spread[CODES] = csm[...].astype(F32)
    for pair in range(size_x // 2):
        parts = [spread[CODES, pl.ds(2 * pair + k, H, stride=size_x), :] for k in range(2)]
        even, odd = even_odd(low[:H], *parts)
        both = jnp.concatenate([even, odd], axis=0).astype(BF16)
        call[depth, pair] = exact_dot(both, order)
    partner = pltpu.make_async_remote_copy(
        src_ref=call.at[depth],
        dst_ref=call.at[depth],
        send_sem=ss_send,
        recv_sem=ss_recv,
        device_id=(track, lateral, 1 - depth),
        device_id_type=MESH,
    )
    fill.wait()

    def sort_fine(half, k):
        i = half * size_x + k
        def block(layer, code):
            return fblk[half][k, table[2 * i + layer, code]]

        for near in range(9):
            code = near * 3 + 1
            one = jnp.where(upper, block(0, code), block(1, code - 1))
            two = jnp.where(upper, block(0, code + 1), block(1, code))
            even, odd = even_odd(low, one, two)
            at = pl.ds(near * 128, 128)
            fine[i, pl.ds(0, B), at] = even
            fine[i, pl.ds(B, B), at] = odd
        mass = fmass[i // 2, lax.rem(i, 2)].astype(F32)
        mass = jnp.concatenate([mass[0:1], mass[1:2]], axis=1)
        diag = jnp.where(fine_order(row) == col, jnp.broadcast_to(mass, (128, 128)), 0.0)
        fine[i, :, pl.ds(9 * 128, 128)] = diag.astype(BF16)
        for source, target, reordering in ((fsm, smooth, swap), (tran, transfer, order)):
            whole = source[i]
            zero = jnp.zeros_like(whole)
            even, odd = even_odd(low, jnp.where(upper, whole, zero), jnp.where(upper, zero, whole))
            target[i] = exact_dot(jnp.concatenate([even, odd], axis=0), reordering)

    for half in range(2):
        def wait_block(i, carry, half=half):
            block_load(half, i).wait()
            return carry

        def sort_step(i, carry, half=half):
            sort_fine(half, i)
            return carry

        lax.fori_loop(0, size_x, wait_block, 0)
        lax.fori_loop(0, size_x, sort_step, 0)
    def apply_fine(sweep, x, y):
        pieces = [
            padded[sweep, x + dx, pl.ds(y, 3)].reshape(3 * 128, LD) for dx in range(3)
        ]
        pieces.append(padded[sweep, x + 1, y + 1])
        return dot(fine[2 * x + y], jnp.concatenate(pieces, axis=0))

    def await_halo(sweep, xs):
        if 0 in xs:
            track_do("wait_recv", sweep, 1)
        if last in xs:
            track_do("wait_recv", sweep, 0)
        for x in ahead[sweep, xs]:
            lateral_do("wait_recv", sweep, x)

    def residuals(sweep, cells):
        totals = [apply_fine(sweep, x, y) for x, y in cells]
        return [(forces[x, y] - t).astype(BF16) for (x, y), t in zip(cells, totals)]

    for sweep in range(SWEEPS):
        for xs in passes[sweep]:
            await_halo(sweep, xs)
            cells = [(x, y) for x in xs for y in range(2)]
            res = residuals(sweep, cells)
            steps = [DAMPING * dot(smooth[2 * x + y], r) for (x, y), r in zip(cells, res)]
            news = [iterate[x, y] + step for (x, y), step in zip(cells, steps)]
            plain = [exact_dot(swap, new.astype(BF16)) for new in news]
            for (x, y), new, rounded in zip(cells, news, plain):
                iterate[x, y] = new
                padded[sweep + 1, x + 1, y + 1] = rounded
            if 0 in xs:
                track_do("start", sweep + 1, 0)
            if last in xs:
                track_do("start", sweep + 1, 1)
            for x in xs:
                lateral_do("start", sweep + 1, x)

    pl.when(depth == 1)(partner.start)
    for xs in passes[SWEEPS]:
        await_halo(SWEEPS, xs)
        cells = [(x, y) for x in xs for y in range(2)]
        for (x, y), r in zip(cells, residuals(SWEEPS, cells)):
            projected[y, x] = lax.dot_general(
                transfer[2 * x + y], r, (((0,), (0,)), ((), ())), preferred_element_type=F32
            )

    @pl.when(depth == 0)
    def _():
        pl.semaphore_wait(ready, size_l + crossing_count)
        partner.start()

    def to_coarse(other_l, other_d):
        r = lax.rem(other_l * 2 + other_d - me + group, group)
        return r, pltpu.make_async_remote_copy(
            src_ref=csend.at[other_l],
            dst_ref=cres.at[depth, lateral],
            send_sem=to_send.at[r],
            recv_sem=to_recv.at[r],
            device_id=(track, other_l, other_d),
            device_id_type=MESH,
        )

    def group_column(i, carry):
        a = lax.rem(lateral + 1 + i, size_x)
        for z in range(2):
            rows = pl.ds(z * B, B)
            total = (
                projected[0, table[5 * size_x + z, a], rows, :]
                + projected[1, table[5 * size_x + 2 + z, a], rows, :]
            )
            csend[a, rows, :] = total.astype(BF16)
        for other_d in range(2):
            r, copy = to_coarse(a, other_d)

            @pl.when(r != 0)
            def _(copy=copy):
                copy.start()
        return carry

    lax.fori_loop(0, size_x, group_column, 0)
    cres[depth, lateral] = csend[lateral]

    clear(cpad, *[(dx, every, y) for dx in range(3) for y in (0, size_l + 1)])
    for index in range(2):
        @pl.when(jnp.logical_not(sides[index][1]))
        def _(index=index):
            clear(cpad, 2 * index)

    def from_fine(y, h):
        r = lax.rem(me - 2 * y - h + group, group)

        @pl.when(r != 0)
        def _():
            pltpu.make_async_remote_copy(
                src_ref=csend.at[y],
                dst_ref=cres.at[h, y],
                send_sem=to_send.at[r],
                recv_sem=to_recv.at[r],
                device_id=(track, y, h),
                device_id_type=MESH,
            ).wait_recv()

    def first_pair(h, pair):
        for k in range(2):
            from_fine(2 * pair + k, h)
        for z in range(2):
            rows = pl.ds(z * B, B)
            stack = [cres[h, 2 * pair + k, rows, :] for k in range(2)]
            block = call[z, pair]
            zero = jnp.zeros_like(block)
            left = jnp.concatenate(
                [jnp.where(low, block, zero), jnp.where(low, zero, block)], axis=0
            )
            value = DAMPING * dot(left, jnp.concatenate(stack, axis=0))
            plain = exact_dot(order, value.astype(BF16))
            for k in range(2):
                first[z, h, 2 * pair + k] = value[k * B : (k + 1) * B]
                cpad[1, h, 2 * pair + k + 1, rows, :] = plain[k * B : (k + 1) * B]

    def side_copy(index, h, pair):
        rows = pl.ds(2 * pair + 1, 2)
        return pltpu.make_async_remote_copy(
            src_ref=cpad.at[1, h, rows],
            dst_ref=cpad.at[2 - 2 * index, h, rows],
            send_sem=side_send.at[index, h, pair],
            recv_sem=side_recv.at[index, h, pair],
            device_id=sides[index][0],
            device_id_type=MESH,
        )

    def first_half(h):
        for pair in range(pairs):
            first_pair(h, pair)
            for index in range(2):
                @pl.when(sides[index][1])
                def _(index=index, pair=pair):
                    side_copy(index, h, pair).start()

    partner.wait()
    first_half(0)

    for load in loads[9:]:
        load.wait()

    def widen(slot, carry):
        spread[slot] = cblk[slot].astype(F32)
        return carry

    lax.fori_loop(0, CODES, widen, 0)

    def sort_coarse(y, carry):
        for near in range(9):
            parts = []
            for z in range(2):
                slot = table[4 * size_x + y, near * 3 + 1 + z - depth]
                parts.append(spread[slot, pl.ds(y, H, stride=size_x), :])
            even, odd = even_odd(low[:H], *parts)
            at = pl.ds(near * 128, 128)
            coarse[y, pl.ds(0, H), at] = even.astype(BF16)
            coarse[y, pl.ds(H, H), at] = odd.astype(BF16)
        chosen = lax.broadcasted_iota(jnp.int32, (size_x, B), 0) == y
        mass = jnp.where(chosen, cmass[...].astype(F32), 0.0)
        mass = jnp.sum(mass, axis=0, keepdims=True)
        mass = jnp.broadcast_to(jnp.concatenate([mass, mass], axis=1), (B, 128))
        wanted = coarse_order(row[:B]) + depth * B
        coarse[y, :, pl.ds(9 * 128, 128)] = jnp.where(wanted == col[:B], mass, 0.0).astype(BF16)
        return carry

    lax.fori_loop(0, size_x, sort_coarse, 0)

    first_half(1)
    def sent_column(x, carry):
        for sweep in range(SWEEPS + 1):
            lateral_do("wait_send", sweep, x)
        return carry

    lax.fori_loop(0, size_x, sent_column, 0)
    for sweep in range(SWEEPS + 1):
        for side in range(2):
            track_do("wait_send", sweep, side)


    own_rows = pl.ds(pl.multiple_of(depth * B, B), B)

    def to_fine(y, h):
        r = lax.rem(2 * y + h - me + group, group)
        return r, pltpu.make_async_remote_copy(
            src_ref=csend_back.at[h, y],
            dst_ref=corr.at[depth, lateral],
            send_sem=back_send.at[r],
            recv_sem=back_recv.at[r],
            device_id=(track, y, h),
            device_id_type=MESH,
        )

    def await_side(h, pair):
        for index in range(2):
            @pl.when(sides[1 - index][1])
            def _(index=index):
                side_copy(index, h, pair).wait_recv()

    for h in range(2):
        await_side(h, 0)
        for pair in range(pairs):
            if pair + 1 < pairs:
                await_side(h, pair + 1)
            ys = (2 * pair, 2 * pair + 1)
            remain = []
            for y in ys:
                pieces = [cpad[dx, h, pl.ds(y, 3)].reshape(3 * 128, LD) for dx in range(3)]
                pieces.append(cpad[1, h, y + 1])
                total = dot(coarse[y], jnp.concatenate(pieces, axis=0))
                remain.append((cres[h, y, own_rows, :].astype(F32) - total).astype(BF16))
            block = call[depth, pair]
            zero = jnp.zeros_like(block)
            left = jnp.concatenate(
                [jnp.where(low, block, zero), jnp.where(low, zero, block)], axis=0
            )
            delta = DAMPING * dot(left, jnp.concatenate(remain, axis=0))
            for k, y in enumerate(ys):
                new = first[depth, h, y] + delta[k * B : (k + 1) * B]
                csend_back[h, y] = new.astype(BF16)
                r, copy = to_fine(y, h)

                @pl.when(r != 0)
                def _(copy=copy):
                    copy.start()

    corr[depth, lateral] = csend_back[depth, lateral]

    for index in range(2):
        for h in range(2):
            for pair in range(pairs):
                @pl.when(sides[index][1])
                def _(index=index, h=h, pair=pair):
                    side_copy(index, h, pair).wait_send()

    def sent_coarse(y, carry):
        for h in range(2):
            r, copy = to_coarse(y, h)

            @pl.when(r != 0)
            def _(copy=copy):
                copy.wait_send()
        return carry

    lax.fori_loop(0, size_l, sent_coarse, 0)

    def from_coarse(x, carry):
        for z in range(2):
            r = lax.rem(me - 2 * x - z + group, group)

            @pl.when(r != 0)
            def _(z=z, r=r):
                pltpu.make_async_remote_copy(
                    src_ref=csend_back.at[z, x],
                    dst_ref=corr.at[z, x],
                    send_sem=back_send.at[r],
                    recv_sem=back_recv.at[r],
                    device_id=(track, x, z),
                    device_id_type=MESH,
                ).wait_recv()
        return carry

    lax.fori_loop(0, size_x, from_coarse, 0)

    def final_column(x, carry):
        for y in range(2):
            parts = [
                corr[z, table[5 * size_x + 4 + 2 * y + z, x]] for z in range(2)
            ]
            iterate[x, y] += dot(transfer[2 * x + y], jnp.concatenate(parts, axis=0))
            for z in range(2):
                for parity in range(2):
                    rows = every_second(parity * B + z)
                    out[x, y, z, every_second(parity), :] = iterate[x, y, rows, :]
        return carry

    lax.fori_loop(0, size_x, final_column, 0)

    def sent_fine(y, carry):
        for h in range(2):
            r, copy = to_fine(y, h)

            @pl.when(r != 0)
            def _(copy=copy):
                copy.wait_send()
        return carry

    lax.fori_loop(0, size_l, sent_fine, 0)


def run_cycle(
    tracks, rhs, start, fine_blocks, fine_cols, fine_mass, fine_smoother, transfer, aggregate,
    coarse_blocks, coarse_cols, coarse_mass, coarse_smoother,
):
    size_x = rhs.shape[0]
    count = 2 * size_x
    group = 2 * size_x
    tiles = B * B // 128
    fine_blocks = fine_blocks.reshape(size_x, 2, 2, CODES, tiles, 128)
    fine_blocks = jnp.transpose(fine_blocks, (0, 1, 3, 4, 2, 5)).reshape(count, CODES, B, 128)
    pair = []
    for array in (fine_smoother, transfer):
        array = jnp.transpose(array.reshape(size_x, 2, 2, tiles, 128), (0, 1, 3, 2, 4))
        pair.append(array.reshape(count, B, 128))
    coarse_blocks = coarse_blocks.reshape(size_x, CODES, tiles, 128)
    coarse_blocks = jnp.transpose(coarse_blocks, (1, 2, 0, 3)).reshape(CODES, tiles * size_x, 128)
    coarse_smoother = jnp.transpose(coarse_smoother.reshape(size_x, tiles, 128), (1, 0, 2))
    coarse_smoother = coarse_smoother.reshape(tiles * size_x, 128)
    operands = (
        rhs, start, fine_blocks, fine_cols.reshape(2 * count, CODES), fine_mass, *pair,
        jnp.transpose(aggregate, (1, 2, 0)).reshape(4, size_x), coarse_blocks,
        coarse_cols.reshape(size_x, CODES), coarse_mass.reshape(size_x, B), coarse_smoother,
    )
    held = [(array.shape, array.dtype) for array in operands]
    held[2:3] = [((size_x, CODES, B, 128), BF16)] * 2
    vmem, dma = pltpu.VMEM, pltpu.SemaphoreType.DMA
    table_rows = 5 * size_x + 8
    pairs = size_x // 2
    return pl.pallas_call(
        functools.partial(cycle_kernel, tracks),
        in_specs=[pl.BlockSpec(memory_space=pl.ANY)] * len(operands),
        out_specs=pl.BlockSpec(memory_space=pltpu.VMEM),
        out_shape=jax.ShapeDtypeStruct(rhs.shape, F32),
        scratch_shapes=[vmem(shape, dtype) for shape, dtype in held] + [
            vmem((table_rows, 128), jnp.int32),
            pltpu.SMEM((table_rows, 128), jnp.int32),
            vmem((count, 128, WIDE), BF16),
            vmem((count, 128, 128), BF16),
            vmem((count, 128, 128), BF16),
            vmem((size_x, B, WIDE), BF16),
            vmem((CODES + 1, tiles * size_x, 128), F32),
            vmem((SWEEPS + 1, size_x + 2, 4, 128, LD), BF16),
            vmem((size_x, 2, 128, LD), F32),
            vmem((size_x, 2, 128, LD), F32),
            vmem((2, size_x, 128, LD), F32),
            vmem((size_x, 128, LD), BF16),
            vmem((2, size_x, 128, LD), BF16),
            vmem((3, 2, size_x + 2, 128, LD), BF16),
            vmem((2, size_x // 2, B, 128), BF16),
            vmem((2, 2, size_x, B, LD), F32),
            vmem((2, size_x, B, LD), BF16),
            vmem((2, size_x, B, LD), BF16),
            dma((11,)), dma((count,)), dma,
            dma((SWEEPS + 1, 2, size_x)), dma((SWEEPS + 1, 2, size_x)),
            dma((SWEEPS + 1, 2, 3)), dma((SWEEPS + 1, 2, 3)),
            dma((group,)), dma((group,)), dma((group,)), dma((group,)),
            dma((2, 2, pairs)), dma((2, 2, pairs)), dma, dma,
            pltpu.SemaphoreType.REGULAR,
        ],
        compiler_params=pltpu.CompilerParams(
            collective_id=0, has_side_effects=True, vmem_limit_bytes=56 << 20
        ),
        name="cycle",
    )(*operands)


def solution(mesh):
    tracks = mesh.shape["track"]

    def per_device(*arrays):
        return run_cycle(tracks, *arrays)

    in_specs = (
        P("track", "lateral", None, None, "depth"),
        P("track", "lateral", None, None, "depth"),
        P("track", "lateral", None, None, None),
        P("track", "lateral", None, None),
        P("track", "lateral", None, None),
        P("track", "lateral", None, None),
        P("track", "lateral", None, None),
        P("track", "lateral", None),
        P(("track", "lateral"), None, "depth", None, None),
        P(("track", "lateral"), None, "depth", None),
        P(("track", "lateral"), None, "depth", None),
        P(("track", "lateral"), None, "depth", None),
    )
    out_specs = P("track", "lateral", None, None, "depth")
    return jax.shard_map(
        per_device, mesh=mesh, in_specs=in_specs, out_specs=out_specs, check_vma=False
    )
```
